32 devices in a mesh: curve: 8 (over z, x), sub: 4 (over y, core).
Axes of the slice: x: 2, y: 2, z: 4, core: 2. Of those that a mesh axis runs over, the one named last changes fastest.
Arguments:
- load: float32 [3, 32, 64, 128], P(None, 'sub', 'curve'), may hold values from -6 to 6
- plastic: float32 [32, 64, 128], P('sub', 'curve'), may hold values from 0 to 0.95, as said below
- tile_material: int32 [4, 8, 16], P('sub', 'curve'), may hold values from 0 to 4
- moduli: float32 [4], replicated, may hold values from 0.5 to 4
- k_vol: float32 [24, 24], replicated
- k_dev: float32 [24, 24], replicated
Outputs:
- solution: float32 [3, 32, 64, 128], P(None, 'sub', 'curve')
- residual: float32 [3, 32, 64, 128], P(None, 'sub', 'curve')
The draws below stay inside these ranges and needn't reach their ends.
Inputs may be any that keep to these rules, and one draw needn't show every extreme that they name: `plastic`: zero for voxels that have not yielded, else the share lost.
All inputs are finite; a program needn't handle non-finite values.
Results may differ from the reference program's by a relative error of at most 0.0003.
Values sent between devices are 32-bit elements; how exact they have to be, the bound alone decides.
No kernel may reach another device: no remote copies, remote signals or barrier semaphores. Data moves between devices by JAX's collectives and lax.ppermute only.
A program may use at most 64 MiB of HBM per device.

```python
import math
import jax
import jax.numpy as jnp
from jax import lax

TILE = 8
TY = 16
MATERIALS = 4
ITERS = 3
NTX = 4
NTZ = 8
NX = 32
NZ = 64
NY = 128


def stiffness_matrix(key):
    first, second = jax.random.split(key, 2)
    raw = jax.random.normal(first, (24, 24), jnp.float32) * 0.35
    symmetric = (raw + raw.T) * 0.5
    symmetric = symmetric - jnp.diag(jnp.diag(symmetric))
    diagonal = jnp.sum(jnp.abs(symmetric), axis=1) + jax.random.uniform(second, (24,), jnp.float32, 0.5, 1.5)
    matrix = symmetric + jnp.diag(diagonal)
    return matrix.astype(jnp.float32)


def draw_k_vol(key, part):
    return stiffness_matrix(jax.random.fold_in(key, 11))


def draw_k_dev(key, part):
    return stiffness_matrix(jax.random.fold_in(key, 23))


def draw_plastic(key, part):
    first, second = jax.random.split(jax.random.fold_in(key, 37))
    shape = (NX, NZ, NY)
    yielded = jax.random.randint(first, shape, 0, 10) < 3
    share = jax.random.uniform(second, shape, jnp.float32, 0.2, 0.9)
    return jnp.where(yielded, share, 0.0).astype(jnp.float32)


def draw_tile_material(key, part):
    first, second = jax.random.split(jax.random.fold_in(key, 53))
    shape = (NTX, NTZ, TY)
    tiles_x = jnp.arange(NTX, dtype=jnp.int32)[:, None, None]
    tiles_y = jnp.arange(TY, dtype=jnp.int32)[None, None, :]
    offset_x = 2 * tiles_x - (NTX - 1)
    offset_y = 2 * tiles_y - (TY - 1)
    inside = offset_x * offset_x * TY * TY + offset_y * offset_y * NTX * NTX <= NTX * NTX * TY * TY
    roll = jax.random.randint(first, shape, 0, 100)
    occupied = jnp.where(inside, roll < 90, roll < 15)
    material = jax.random.randint(second, shape, 1, MATERIALS + 1)
    return jnp.where(occupied, material, 0).astype(jnp.int32)


def shard_levels(stream_key, dims, cuts, low, high):
    def one(axis_at, blocks):
        steps = jax.random.uniform(jax.random.fold_in(jax.random.fold_in(stream_key, 6), axis_at), (blocks,), jnp.float32, low / len(cuts), high / len(cuts))
        return jnp.repeat(jnp.exp(steps), dims[axis_at] // blocks).reshape((-1,) + (1,) * (len(dims) - axis_at - 1))

    gain = one(*cuts[0])
    for cut in cuts[1:]:
        gain = gain * one(*cut)
    return gain


def scatter_about(rng, shape, spread, reach, cuts=(), held_as=jnp.bfloat16):
    entries = jax.random.normal(rng, shape, jnp.float32) * spread
    if len(cuts) > 0:
        entries = shard_levels(rng, shape, cuts, -0.22, 0.18) * entries
    return jnp.clip(entries, min=-reach, max=reach).astype(held_as)


def setup_inputs(seed: int = 0) -> dict:
    seeds = jax.random.split(jax.random.key(seed), 7)
    load = scatter_about(seeds[0], (3, NX, NZ, NY), 1.0, 6.0, ((1, 4), (2, 8)), jnp.float32)
    plastic = draw_plastic(jax.random.fold_in(seeds[6], 71), 0)
    tile_material = draw_tile_material(jax.random.fold_in(seeds[6], 71), 0)
    moduli = jnp.clip(jnp.exp(jax.random.uniform(seeds[3], (MATERIALS,), jnp.float32, math.log(0.5), math.log(4.0))), 0.5, 4.0)
    k_vol = draw_k_vol(jax.random.fold_in(seeds[6], 71), 0)
    k_dev = draw_k_dev(jax.random.fold_in(seeds[6], 71), 0)
    return {"load": load, "plastic": plastic, "tile_material": tile_material, "moduli": moduli, "k_vol": k_vol, "k_dev": k_dev}


ground_spring = 0.5


def voxel_coefficients(tile_material, moduli, plastic):
    one_hot = (tile_material[..., None] == jnp.arange(1, MATERIALS + 1, dtype=jnp.int32)).astype(jnp.float32)
    tile_modulus = jnp.sum(one_hot * moduli, axis=-1)
    voxel_modulus = jnp.repeat(jnp.repeat(jnp.repeat(tile_modulus, TILE, 0), TILE, 1), TILE, 2)
    return jnp.stack([voxel_modulus, voxel_modulus * (1.0 - plastic)])


def shift_second(values, along_y):
    if along_y == 0:
        return values
    zeros_col = jnp.zeros(values.shape[:-1] + (1,), values.dtype)
    return jnp.concatenate([zeros_col, values[..., :-1]], axis=-1)


def keep_mask(extended, first_x, first_z):
    size_x = extended.shape[1] - 1
    size_z = extended.shape[2] - 1
    size_y = extended.shape[3]
    occupied = (extended[0] > 0).astype(jnp.float32)
    active = jnp.zeros((size_x, size_z, size_y), jnp.float32)
    for along_x in (0, 1):
        for along_z in (0, 1):
            for along_y in (0, 1):
                contrib = occupied[1 - along_x:1 - along_x + size_x, 1 - along_z:1 - along_z + size_z, :]
                active = jnp.maximum(active, shift_second(contrib, along_y))
    index_x = first_x + jnp.arange(size_x, dtype=jnp.int32)
    index_z = first_z + jnp.arange(size_z, dtype=jnp.int32)
    index_y = jnp.arange(size_y, dtype=jnp.int32)
    free = (index_x > 0)[:, None, None] & (index_z > 0)[None, :, None] & (index_y > 0)[None, None, :]
    return active * free.astype(jnp.float32)


def node_forces(bordered, extended, k_vol, k_dev):
    size_x = extended.shape[1] - 1
    size_z = extended.shape[2] - 1
    size_y = extended.shape[3]
    lower = jnp.moveaxis(bordered[:, 0:size_x + 1], 1, 0)
    upper = jnp.moveaxis(bordered[:, 1:size_x + 2], 1, 0)
    layer_coef = jnp.moveaxis(extended, 1, 0)

    def assemble(forces, along_x):
        summed = jnp.zeros((3, size_z, size_y), jnp.float32)
        for along_z in (0, 1):
            for along_y in (0, 1):
                contrib = forces[along_x * 4 + along_z * 2 + along_y][:, 1 - along_z:1 - along_z + size_z, :]
                summed = summed + shift_second(contrib, along_y)
        return summed

    def layer(carried, layer_item):
        lower_nodes, upper_nodes, coef_layer = layer_item
        corners = []
        for source in (lower_nodes, upper_nodes):
            for along_z in (0, 1):
                block = source[:, along_z:along_z + size_z + 1, :]
                corners.append(block)
                zeros_col = jnp.zeros((3, size_z + 1, 1), jnp.float32)
                corners.append(jnp.concatenate([block[:, :, 1:], zeros_col], axis=2))
        element = jnp.concatenate(corners, 0).reshape(24, (size_z + 1) * size_y)
        vol_scale = coef_layer[0].reshape(1, -1)
        dev_scale = coef_layer[1].reshape(1, -1)
        forces = jnp.dot(k_vol, vol_scale * element, precision=lax.Precision.HIGHEST, preferred_element_type=jnp.float32)
        forces = forces + jnp.dot(k_dev, dev_scale * element, precision=lax.Precision.HIGHEST, preferred_element_type=jnp.float32)
        forces = forces.reshape(8, 3, size_z + 1, size_y)
        return assemble(forces, 1), carried + assemble(forces, 0)

    start = jnp.zeros((3, size_z, size_y), jnp.float32)
    _, emitted = lax.scan(layer, start, (lower, upper, layer_coef))
    return jnp.moveaxis(emitted[1:], 0, 1)


def reference(load, plastic, tile_material, moduli, k_vol, k_dev):
    coefficients = voxel_coefficients(tile_material, moduli, plastic)
    extended = jnp.pad(coefficients, ((0, 0), (1, 0), (1, 0), (0, 0)))
    keep = keep_mask(extended, 0, 0)

    def operate(field_vals):
        bordered = jnp.pad(field_vals, ((0, 0), (1, 1), (1, 1), (0, 0)))
        return keep * (node_forces(bordered, extended, k_vol, k_dev) + ground_spring * field_vals)

    residual = keep * load
    solution = jnp.zeros_like(residual)
    image = operate(residual)
    norm_now = jnp.sum(residual * residual)
    curvature = jnp.sum(residual * image)
    step_size = norm_now / curvature
    direction = residual
    carried = image
    for iteration in range(ITERS):
        solution = solution + step_size * direction
        residual = residual - step_size * carried
        if iteration + 1 < ITERS:
            image = operate(residual)
            norm_next = jnp.sum(residual * residual)
            curvature = jnp.sum(residual * image)
            next_ratio = norm_next / norm_now
            step_size = norm_next / (curvature - next_ratio * norm_next / step_size)
            direction = residual + next_ratio * direction
            carried = image + next_ratio * carried
            norm_now = norm_next
    return solution, residual
```

```python
import functools

import jax
import jax.numpy as jnp
from jax import lax
from jax.experimental import pallas as pl
from jax.experimental.pallas import tpu as pltpu
from jax.sharding import PartitionSpec as P

TILE = 8
MATERIALS = 4
ITERS = 3
HALO = ITERS

ground_spring = 0.5

AXES = ("curve", "sub")
PAIRS = ((0, 0), (0, 1), (0, 2), (0, 3), (1, 1), (1, 2), (1, 3), (2, 2), (2, 3))


def round_up(value, to):
    return -(-value // to) * to


def exchange(value, axis, first):
    count = lax.axis_size(axis)
    pairs = []
    for i in range(first, count - 1, 2):
        pairs += [(i, i + 1), (i + 1, i)]
    return lax.ppermute(value, axis, pairs)


def is_odd(axis):
    return lax.axis_index(axis) % 2 == 1


def sub_message_kernel(
    dims, tile_ref, moduli_ref, load_ref, plastic_ref, kv_ref, kd_ref, a_ref, b_ref, modulus_ref, k_ref, scale_ref
):
    nx, nz, ny, tx, tz, ty = dims
    odd = is_odd("sub")
    lane = lax.broadcasted_iota(jnp.int32, (1, ny), 1) // TILE
    for t in range(tx * tz):
        row = jnp.zeros((1, ny), jnp.float32)
        for y in range(ty):
            material = tile_ref[t // tz, t % tz, y]
            value = jnp.float32(0)
            for m in range(MATERIALS):
                value = jnp.where(material == m + 1, moduli_ref[m], value)
            row = jnp.where(lane == y, value, row)
        modulus_ref[t : t + 1, :] = row
    span = HALO * nz

    def put(at, low, high):
        rows = low.shape[0]
        a_ref[at : at + rows, :] = jnp.where(odd, low, high)
        b_ref[at : at + rows, :] = jnp.where(odd, high, low)

    for c in range(3):
        base = c * nx * nz
        put(c * span, load_ref[base : base + span, :], load_ref[base + nx * nz - span : base + nx * nz, :])
    put(3 * span, plastic_ref[0:span, :], plastic_ref[nx * nz - span : nx * nz, :])
    put(4 * span, modulus_ref[0:tz, :], modulus_ref[(tx - 1) * tz : tx * tz, :])

    r32 = lax.broadcasted_iota(jnp.int32, (32, 24), 0)
    m32 = lax.broadcasted_iota(jnp.int32, (32, 24), 1)
    spread_rows = ((m32 == 6 * (r32 // 8) + r32 % 8) & (r32 % 8 < 6)).astype(jnp.bfloat16)
    m24 = lax.broadcasted_iota(jnp.int32, (24, 128), 0)
    n24 = lax.broadcasted_iota(jnp.int32, (24, 128), 1)
    target = (m24 == 6 * (n24 % 64 // 16) + n24 % 8) & (n24 % 8 < 6)
    first_cols = (target & (n24 < 64)).astype(jnp.bfloat16)
    second_cols = (target & (n24 >= 64)).astype(jnp.bfloat16)
    dot = functools.partial(jnp.dot, preferred_element_type=jnp.float32)
    for at, ref in ((0, kv_ref), (32, kd_ref)):
        k = ref[...]
        high = k.astype(jnp.bfloat16)
        low = (k - high.astype(jnp.float32)).astype(jnp.bfloat16)
        part = dot(dot(spread_rows, high).astype(jnp.bfloat16), first_cols)
        part = part + dot(dot(spread_rows, low).astype(jnp.bfloat16), second_cols)
        k_ref[at : at + 32, :] = part.astype(jnp.bfloat16)

    def size(k):
        top = jnp.max(jnp.abs(k), axis=(0, 1), keepdims=True)
        safe = jnp.where(top > 0, top, 1.0)
        return top * jnp.sqrt(jnp.sum((k / safe) ** 2, axis=(0, 1), keepdims=True) * (1.0 / 24))

    mean_modulus = jnp.float32(0)
    for m in range(MATERIALS):
        mean_modulus = mean_modulus + moduli_ref[m] * (1.0 / MATERIALS)
    theta = ground_spring + 6.4 * mean_modulus * (size(kv_ref[...]) + 0.85 * size(kd_ref[...]))
    scale_ref[...] = jnp.broadcast_to(1.0 / theta, (8, 128))


def pick(ref_a, ref_b, odd, low_ref, high_ref):
    a = ref_a[...]
    b = ref_b[...]
    low_ref[...] = jnp.where(odd, a, b)
    high_ref[...] = jnp.where(odd, b, a)


def curve_message_kernel(
    dims, load_ref, plastic_ref, modulus_ref, ra_ref, rb_ref, a_ref, b_ref, low_ref, high_ref
):
    nx, nz, ny, tx, tz, ty = dims
    size_x = nx + 2 * HALO
    pick(ra_ref, rb_ref, is_odd("sub"), low_ref, high_ref)
    odd = is_odd("curve")
    for out_ref, z_first, tile_z in (
        (a_ref, jnp.where(odd, 0, nz - HALO), jnp.where(odd, 0, tz - 1)),
        (b_ref, jnp.where(odd, nz - HALO, 0), jnp.where(odd, tz - 1, 0)),
    ):
        for f in range(4):
            for zl in range(HALO):
                at = (f * HALO + zl) * size_x
                z = z_first + zl
                if f < 3:
                    own = load_ref[pl.ds(f * nx * nz + z, nx, stride=nz), :]
                else:
                    own = plastic_ref[pl.ds(z, nx, stride=nz), :]
                side = f * HALO * nz
                out_ref[at : at + HALO, :] = low_ref[pl.ds(side + z, HALO, stride=nz), :]
                out_ref[at + HALO : at + HALO + nx, :] = own
                out_ref[at + HALO + nx : at + size_x, :] = high_ref[pl.ds(side + z, HALO, stride=nz), :]
        at = 4 * HALO * size_x
        row = low_ref[pl.ds(4 * HALO * nz + tile_z, 1), :]
        out_ref[at : at + HALO, :] = jnp.broadcast_to(row, (HALO, ny))
        for t in range(tx):
            row = modulus_ref[pl.ds(t * tz + tile_z, 1), :]
            first = at + HALO + t * TILE
            out_ref[first : first + TILE, :] = jnp.broadcast_to(row, (TILE, ny))
        row = high_ref[pl.ds(4 * HALO * nz + tile_z, 1), :]
        out_ref[at + HALO + nx : at + size_x, :] = jnp.broadcast_to(row, (HALO, ny))


def product_kernel(
    dims,
    load_ref, plastic_ref, modulus_ref, sa_ref, sb_ref, ca_ref, cb_ref, k_ref, scale_ref,
    w0_ref, w1_ref, w2_ref, w3_ref, gram_ref,
    slow_ref, shigh_ref, clow_ref, chigh_ref, vol_ref, dev_ref, keep_ref, field_ref, split_ref, sum_ref,
):
    nx, nz, ny, tx, tz, ty = dims
    size_x = nx + 2 * HALO
    size_z = nz + 2 * HALO
    pitch = round_up(size_z, 8)
    w_refs = (w0_ref, w1_ref, w2_ref, w3_ref)
    pick(sa_ref, sb_ref, is_odd("sub"), slow_ref, shigh_ref)
    pick(ca_ref, cb_ref, is_odd("curve"), clow_ref, chigh_ref)

    for x in range(size_x - 1):
        if x < HALO:
            source, at, e_row = slow_ref, 3 * HALO * nz + x * nz, 4 * HALO * nz
            e_ref = slow_ref
        elif x < HALO + nx:
            source, at, e_row = plastic_ref, (x - HALO) * nz, (x - HALO) // TILE * tz
            e_ref = modulus_ref
        else:
            source, at, e_row = shigh_ref, 3 * HALO * nz + (x - HALO - nx) * nz, 4 * HALO * nz
            e_ref = shigh_ref
        row = x * pitch + HALO
        dev_ref[row : row + nz, :] = source[at : at + nz, :]
        for t in range(tz):
            value = jnp.broadcast_to(e_ref[e_row + t : e_row + t + 1, :], (TILE, ny))
            vol_ref[row + t * TILE : row + (t + 1) * TILE, :] = value
    for zl in range(HALO):
        for ref, z in ((clow_ref, zl), (chigh_ref, HALO + nz + zl)):
            at = (3 * HALO + zl) * size_x
            dev_ref[pl.ds(z, size_x, stride=pitch), :] = ref[at : at + size_x, :]
            at = 4 * HALO * size_x
            vol_ref[pl.ds(z, size_x, stride=pitch), :] = ref[at : at + size_x, :]
    first_lane = lax.broadcasted_iota(jnp.int32, (8, ny), 1) == 0
    last_lane = lax.broadcasted_iota(jnp.int32, (8, ny), 1) == ny - 1

    x_index = lax.axis_index("sub") * nx - HALO
    x_count = lax.axis_size("sub") * nx
    z_row = lax.broadcasted_iota(jnp.int32, (pitch, ny), 0) + (lax.axis_index("curve") * nz - HALO)
    z_free = (z_row > 0) & (z_row < lax.axis_size("curve") * nz)
    y_free = lax.broadcasted_iota(jnp.int32, (pitch, ny), 1) > 0
    free = (z_free & y_free).astype(jnp.float32)
    row_index = lax.broadcasted_iota(jnp.int32, (pitch, ny), 0)
    for x in range(size_x):
        below = max(x - 1, 0) * pitch
        above = min(x, size_x - 2) * pitch
        e = jnp.maximum(vol_ref[below : below + pitch, :], vol_ref[above : above + pitch, :])
        e = jnp.where(row_index < size_z - 1, e, pltpu.roll(e, 1, 0))
        before = jnp.where(row_index == 0, e, pltpu.roll(e, 1, 0))
        e = jnp.maximum(e, before)
        e = jnp.maximum(e, pltpu.roll(e, 1, 1))
        here = x_index + x
        x_free = jnp.where((here > 0) & (here < x_count), 1.0, 0.0)
        keep_ref[x * pitch : (x + 1) * pitch, :] = jnp.where(e > 0, free * x_free, 0.0)
    for x in range(size_x - 1):
        rows = pl.ds(x * pitch, pitch)
        dev_ref[rows, :] = vol_ref[rows, :] * (1.0 - dev_ref[rows, :])

    def store_node(x, z, value):
        ahead = jnp.where(last_lane, 0.0, pltpu.roll(value, ny - 1, 1))
        both = value + pltpu.roll(ahead, 3, 0)
        field_ref[x, :, z * ny : (z + 1) * ny] = value
        high = both.astype(jnp.bfloat16).astype(jnp.float32)
        split_ref[x, :, z * ny : (z + 1) * ny] = jnp.concatenate([high, both - high], axis=0).astype(jnp.bfloat16)

    blank = jnp.zeros((5, ny), jnp.float32)
    for x in range(size_x):
        for z in range(size_z):
            if z < HALO:
                rows = clow_ref[pl.ds(z * size_x + x, 3, stride=HALO * size_x), :]
            elif z >= HALO + nz:
                rows = chigh_ref[pl.ds((z - HALO - nz) * size_x + x, 3, stride=HALO * size_x), :]
            elif x < HALO:
                rows = slow_ref[pl.ds(x * nz + z - HALO, 3, stride=HALO * nz), :]
            elif x >= HALO + nx:
                rows = shigh_ref[pl.ds((x - HALO - nx) * nz + z - HALO, 3, stride=HALO * nz), :]
            else:
                rows = load_ref[pl.ds((x - HALO) * nz + z - HALO, 3, stride=nx * nz), :]
            value = jnp.concatenate([rows, blank], axis=0) * keep_ref[pl.ds(x * pitch + z, 1), :]
            store_node(x, z, value)

    def save(out_ref):
        for x in range(nx):
            for z in range(nz):
                value = field_ref[x + HALO, 0:3, (z + HALO) * ny : (z + HALO + 1) * ny]
                out_ref[pl.ds(x * nz + z, 3, stride=nx * nz), :] = value

    save(w0_ref)
    kmat = k_ref[...]
    inverse = scale_ref[0:1, 0:1]
    component = (lax.broadcasted_iota(jnp.int32, (8, ny), 0) < 3).astype(jnp.float32) * inverse

    for k in range(1, ITERS + 1):
        sum_ref[...] = jnp.zeros_like(sum_ref)

        def layer(i, _, k=k):
            z = k - 1
            end = size_z - k
            side_low = side_high = None
            while z < end:
                cols = min(2, end - z)
                lanes = cols * ny
                parts = []
                for a in (0, 1):
                    for c in (0, 1):
                        parts.append(split_ref[i + a, :, (z + c) * ny : (z + c) * ny + lanes])
                rhs = jnp.concatenate(parts + parts, axis=0)
                forces = jnp.dot(kmat, rhs, preferred_element_type=jnp.float32)
                for j in range(cols):
                    here = z + j
                    vol = vol_ref[pl.ds(i * pitch + here, 1), :]
                    dev = dev_ref[pl.ds(i * pitch + here, 1), :]
                    g = []
                    for q in range(4):
                        f_vol = forces[8 * q : 8 * q + 8, j * ny : (j + 1) * ny]
                        f_dev = forces[32 + 8 * q : 40 + 8 * q, j * ny : (j + 1) * ny]
                        g.append(vol * f_vol + dev * f_dev)
                    if here >= k:
                        span = slice(here * ny, (here + 1) * ny)
                        total = sum_ref[:, span] + (g[0] + side_low)
                        sum_ref[:, span] = g[2] + side_high
                        behind = jnp.where(first_lane, 0.0, pltpu.roll(total, 1, 1))
                        total = total + pltpu.roll(behind, 5, 0)
                        old = field_ref[i, :, span]
                        keep = keep_ref[pl.ds(i * pitch + here, 1), :]
                        store_node(i, here, old - (component * keep) * (total + ground_spring * old))
                    side_low, side_high = g[1], g[3]
                z += cols
            return 0

        lax.fori_loop(k - 1, size_x - k, layer, 0)
        save(w_refs[k])

    sums = [jnp.zeros((8, ny), jnp.float32) for _ in PAIRS]
    for r in range(3 * nx * nz // 8):
        w = [ref[8 * r : 8 * r + 8, :] for ref in w_refs]
        for n, (i, j) in enumerate(PAIRS):
            sums[n] = sums[n] + w[i] * w[j]
    lane = lax.broadcasted_iota(jnp.int32, (1, ny), 1)
    row = jnp.zeros((1, ny), jnp.float32)
    for n, value in enumerate(sums):
        row = jnp.where(lane == n, jnp.sum(value, axis=(0, 1), keepdims=True), row)
    gram_ref[...] = jnp.broadcast_to(row[None], gram_ref.shape)


def finish_kernel(gram_ref, scale_ref, w0_ref, w1_ref, w2_ref, w3_ref, solution_ref, residual_ref):
    total = jnp.sum(gram_ref[...], axis=0)
    lane = lax.broadcasted_iota(jnp.int32, total.shape, 1)
    gram = {}
    for n, (i, j) in enumerate(PAIRS):
        value = jnp.sum(jnp.where(lane == n, total, 0.0), axis=1, keepdims=True)
        gram[i, j] = gram[j, i] = value

    def inner(p, q):
        result = None
        for i, left in enumerate(p):
            for j, right in enumerate(q):
                if left is not None and right is not None:
                    term = left * right * gram[i, j]
                    result = term if result is None else result + term
        return result

    def axpy(p, scale, q):
        out = []
        for left, right in zip(p, q):
            if right is None:
                out.append(left)
            else:
                out.append(scale * right if left is None else left + scale * right)
        return out

    def image_of(p):
        out = []
        for i in range(ITERS + 1):
            here = p[i]
            before = p[i - 1] if i > 0 else None
            if here is None:
                out.append(None if before is None else -before)
            else:
                out.append(here if before is None else here - before)
        return out

    one = jnp.ones((1, 1), jnp.float32)
    solution = [None] * (ITERS + 1)
    residual = [one] + [None] * ITERS
    image = image_of(residual)
    norm_now = inner(residual, residual)
    step = norm_now / inner(residual, image)
    direction = residual
    carried = image
    for iteration in range(ITERS):
        solution = axpy(solution, step, direction)
        residual = axpy(residual, -step, carried)
        if iteration + 1 < ITERS:
            image = image_of(residual)
            norm_next = inner(residual, residual)
            curvature = inner(residual, image)
            ratio = norm_next / norm_now
            step = norm_next / (curvature - ratio * norm_next / step)
            direction = axpy(residual, ratio, direction)
            carried = axpy(image, ratio, carried)
            norm_now = norm_next
    inverse = scale_ref[0:1, 0:1]
    w_refs = (w0_ref, w1_ref, w2_ref, w3_ref)
    solution = [None if c is None else c * inverse for c in solution]
    for out_ref, coefs in ((solution_ref, solution), (residual_ref, residual)):
        value = None
        for c, ref in zip(coefs, w_refs):
            if c is not None:
                value = c * ref[...] if value is None else value + c * ref[...]
        out_ref[...] = value


def local(load, plastic, tile_material, moduli, k_vol, k_dev):
    nx, nz, ny = plastic.shape
    dims = (nx, nz, ny) + tile_material.shape
    tx, tz = tile_material.shape[:2]
    f32 = jnp.float32
    vmem = pl.BlockSpec(memory_space=pltpu.VMEM)
    smem = pl.BlockSpec(memory_space=pltpu.SMEM)
    shape = jax.ShapeDtypeStruct
    load = load.reshape(3 * nx * nz, ny)
    plastic = plastic.reshape(nx * nz, ny)
    size_x = nx + 2 * HALO
    size_z = nz + 2 * HALO
    pitch = round_up(size_z, 8)
    sub_rows = round_up(4 * HALO * nz + tz, 8)
    curve_rows = round_up((4 * HALO + 1) * size_x, 8)
    count = lax.axis_size("curve") * lax.axis_size("sub")

    sub_a, sub_b, modulus, k_both, scale = pl.pallas_call(
        functools.partial(sub_message_kernel, dims),
        out_shape=(
            shape((sub_rows, ny), f32), shape((sub_rows, ny), f32), shape((round_up(tx * tz, 8), ny), f32),
            shape((64, 128), jnp.bfloat16), shape((8, 128), f32),
        ),
        in_specs=[smem, smem, vmem, vmem, vmem, vmem],
        out_specs=(vmem,) * 5,
        name="sub_message",
    )(tile_material, moduli, load, plastic, k_vol, k_dev)
    sub_a = exchange(sub_a, "sub", 0)
    sub_b = exchange(sub_b, "sub", 1)
    curve_a, curve_b = pl.pallas_call(
        functools.partial(curve_message_kernel, dims),
        out_shape=(shape((curve_rows, ny), f32),) * 2,
        in_specs=[vmem] * 5,
        out_specs=(vmem,) * 2,
        scratch_shapes=[pltpu.VMEM((sub_rows, ny), f32)] * 2,
        name="curve_message",
    )(load, plastic, modulus, sub_a, sub_b)
    curve_a = exchange(curve_a, "curve", 0)
    curve_b = exchange(curve_b, "curve", 1)
    *basis, gram = pl.pallas_call(
        functools.partial(product_kernel, dims),
        out_shape=(shape((3 * nx * nz, ny), f32),) * (ITERS + 1) + (shape((count, 1, ny), f32),),
        in_specs=[vmem] * 9,
        out_specs=(vmem,) * (ITERS + 2),
        scratch_shapes=[
            pltpu.VMEM((sub_rows, ny), f32), pltpu.VMEM((sub_rows, ny), f32),
            pltpu.VMEM((curve_rows, ny), f32), pltpu.VMEM((curve_rows, ny), f32),
            pltpu.VMEM((size_x * pitch, ny), f32), pltpu.VMEM((size_x * pitch, ny), f32),
            pltpu.VMEM((size_x * pitch, ny), f32),
            pltpu.VMEM((size_x, 8, size_z * ny), f32),
            pltpu.VMEM((size_x, 16, size_z * ny), jnp.bfloat16),
            pltpu.VMEM((8, size_z * ny), f32),
        ],
        name="products",
    )(load, plastic, modulus, sub_a, sub_b, curve_a, curve_b, k_both, scale)
    gram = lax.all_to_all(gram, AXES, 0, 0)
    solution_out, residual_out = pl.pallas_call(
        finish_kernel,
        out_shape=(shape((3 * nx * nz, ny), f32),) * 2,
        in_specs=[vmem] * 6,
        out_specs=(vmem,) * 2,
        name="finish",
    )(gram, scale, *basis)
    return solution_out.reshape(3, nx, nz, ny), residual_out.reshape(3, nx, nz, ny)


def solution(mesh):
    in_specs = (
        P(None, "sub", "curve", None),
        P("sub", "curve", None),
        P("sub", "curve", None),
        P(),
        P(),
        P(),
    )
    out_specs = (P(None, "sub", "curve", None), P(None, "sub", "curve", None))
    return jax.shard_map(local, mesh=mesh, in_specs=in_specs, out_specs=out_specs, check_vma=False)
```

```python
import functools

import jax
import jax.numpy as jnp
from jax import lax
from jax.experimental import pallas as pl
from jax.experimental.pallas import tpu as pltpu
from jax.sharding import PartitionSpec as P

TILE = 8
MATERIALS = 4
ITERS = 3
HALO = ITERS

ground_spring = 0.5

AXES = ("curve", "sub")
PAIRS = ((0, 0), (0, 1), (0, 2), (0, 3), (1, 1), (1, 2), (1, 3), (2, 2), (2, 3))


def round_up(value, to):
    return -(-value // to) * to


def exchange(value, axis, first):
    count = lax.axis_size(axis)
    pairs = []
    for i in range(first, count - 1, 2):
        pairs += [(i, i + 1), (i + 1, i)]
    return lax.ppermute(value, axis, pairs)


def is_odd(axis):
    return lax.axis_index(axis) % 2 == 1


def sub_message_kernel(
    dims, tile_ref, moduli_ref, load_ref, plastic_ref, kv_ref, kd_ref, a_ref, b_ref, modulus_ref, k_ref, scale_ref
):
    nx, nz, ny, tx, tz, ty = dims
    odd = is_odd("sub")
    lane = lax.broadcasted_iota(jnp.int32, (1, ny), 1) // TILE
    for t in range(tx * tz):
        row = jnp.zeros((1, ny), jnp.float32)
        for y in range(ty):
            material = tile_ref[t // tz, t % tz, y]
            value = jnp.float32(0)
            for m in range(MATERIALS):
                value = jnp.where(material == m + 1, moduli_ref[m], value)
            row = jnp.where(lane == y, value, row)
        modulus_ref[t : t + 1, :] = row
    span = HALO * nz

    def put(at, low, high):
        rows = low.shape[0]
        a_ref[at : at + rows, :] = jnp.where(odd, low, high)
        b_ref[at : at + rows, :] = jnp.where(odd, high, low)

    for c in range(3):
        base = c * nx * nz
        put(c * span, load_ref[base : base + span, :], load_ref[base + nx * nz - span : base + nx * nz, :])
    put(3 * span, plastic_ref[0:span, :], plastic_ref[nx * nz - span : nx * nz, :])
    put(4 * span, modulus_ref[0:tz, :], modulus_ref[(tx - 1) * tz : tx * tz, :])

    r32 = lax.broadcasted_iota(jnp.int32, (32, 24), 0)
    m32 = lax.broadcasted_iota(jnp.int32, (32, 24), 1)
    spread_rows = ((m32 == 6 * (r32 // 8) + r32 % 8) & (r32 % 8 < 6)).astype(jnp.bfloat16)
    m24 = lax.broadcasted_iota(jnp.int32, (24, 128), 0)
    n24 = lax.broadcasted_iota(jnp.int32, (24, 128), 1)
    target = (m24 == 6 * (n24 % 64 // 16) + n24 % 8) & (n24 % 8 < 6)
    first_cols = (target & (n24 < 64)).astype(jnp.bfloat16)
    second_cols = (target & (n24 >= 64)).astype(jnp.bfloat16)
    dot = functools.partial(jnp.dot, preferred_element_type=jnp.float32)
    for at, ref in ((0, kv_ref), (32, kd_ref)):
        k = ref[...]
        high = k.astype(jnp.bfloat16)
        low = (k - high.astype(jnp.float32)).astype(jnp.bfloat16)
        part = dot(dot(spread_rows, high).astype(jnp.bfloat16), first_cols)
        part = part + dot(dot(spread_rows, low).astype(jnp.bfloat16), second_cols)
        k_ref[at : at + 32, :] = part.astype(jnp.bfloat16)

    def size(k):
        top = jnp.max(jnp.abs(k), axis=(0, 1), keepdims=True)
        safe = jnp.where(top > 0, top, 1.0)
        return top * jnp.sqrt(jnp.sum((k / safe) ** 2, axis=(0, 1), keepdims=True) * (1.0 / 24))

    mean_modulus = jnp.float32(0)
    for m in range(MATERIALS):
        mean_modulus = mean_modulus + moduli_ref[m] * (1.0 / MATERIALS)
    theta = ground_spring + 6.4 * mean_modulus * (size(kv_ref[...]) + 0.85 * size(kd_ref[...]))
    scale_ref[...] = jnp.broadcast_to(1.0 / theta, (8, 128))


def pick(ref_a, ref_b, odd, low_ref, high_ref):
    a = ref_a[...]
    b = ref_b[...]
    low_ref[...] = jnp.where(odd, a, b)
    high_ref[...] = jnp.where(odd, b, a)


def curve_message_kernel(
    dims, load_ref, plastic_ref, modulus_ref, ra_ref, rb_ref, a_ref, b_ref, low_ref, high_ref
):
    nx, nz, ny, tx, tz, ty = dims
    size_x = nx + 2 * HALO
    pick(ra_ref, rb_ref, is_odd("sub"), low_ref, high_ref)
    odd = is_odd("curve")
    for out_ref, z_first, tile_z in (
        (a_ref, jnp.where(odd, 0, nz - HALO), jnp.where(odd, 0, tz - 1)),
        (b_ref, jnp.where(odd, nz - HALO, 0), jnp.where(odd, tz - 1, 0)),
    ):
        for f in range(4):
            for zl in range(HALO):
                at = (f * HALO + zl) * size_x
                z = z_first + zl
                if f < 3:
                    own = load_ref[pl.ds(f * nx * nz + z, nx, stride=nz), :]
                else:
                    own = plastic_ref[pl.ds(z, nx, stride=nz), :]
                side = f * HALO * nz
                out_ref[at : at + HALO, :] = low_ref[pl.ds(side + z, HALO, stride=nz), :]
                out_ref[at + HALO : at + HALO + nx, :] = own
                out_ref[at + HALO + nx : at + size_x, :] = high_ref[pl.ds(side + z, HALO, stride=nz), :]
        at = 4 * HALO * size_x
        row = low_ref[pl.ds(4 * HALO * nz + tile_z, 1), :]
        out_ref[at : at + HALO, :] = jnp.broadcast_to(row, (HALO, ny))
        for t in range(tx):
            row = modulus_ref[pl.ds(t * tz + tile_z, 1), :]
            first = at + HALO + t * TILE
            out_ref[first : first + TILE, :] = jnp.broadcast_to(row, (TILE, ny))
        row = high_ref[pl.ds(4 * HALO * nz + tile_z, 1), :]
        out_ref[at + HALO + nx : at + size_x, :] = jnp.broadcast_to(row, (HALO, ny))


def product_kernel(
    dims,
    load_ref, plastic_ref, modulus_ref, sa_ref, sb_ref, ca_ref, cb_ref, k_ref, scale_ref,
    w0_ref, w1_ref, w2_ref, w3_ref, gram_ref,
    slow_ref, shigh_ref, clow_ref, chigh_ref, vol_ref, dev_ref, keep_ref, field_ref, split_ref, sum_ref,
):
    nx, nz, ny, tx, tz, ty = dims
    size_x = nx + 2 * HALO
    size_z = nz + 2 * HALO
    pitch = round_up(size_z, 8)
    w_refs = (w0_ref, w1_ref, w2_ref, w3_ref)
    pick(sa_ref, sb_ref, is_odd("sub"), slow_ref, shigh_ref)
    pick(ca_ref, cb_ref, is_odd("curve"), clow_ref, chigh_ref)

    for x in range(size_x - 1):
        if x < HALO:
            source, at, e_row = slow_ref, 3 * HALO * nz + x * nz, 4 * HALO * nz
            e_ref = slow_ref
        elif x < HALO + nx:
            source, at, e_row = plastic_ref, (x - HALO) * nz, (x - HALO) // TILE * tz
            e_ref = modulus_ref
        else:
            source, at, e_row = shigh_ref, 3 * HALO * nz + (x - HALO - nx) * nz, 4 * HALO * nz
            e_ref = shigh_ref
        row = x * pitch + HALO
        dev_ref[row : row + nz, :] = source[at : at + nz, :]
        for t in range(tz):
            value = jnp.broadcast_to(e_ref[e_row + t : e_row + t + 1, :], (TILE, ny))
            vol_ref[row + t * TILE : row + (t + 1) * TILE, :] = value
    for zl in range(HALO):
        for ref, z in ((clow_ref, zl), (chigh_ref, HALO + nz + zl)):
            at = (3 * HALO + zl) * size_x
            dev_ref[pl.ds(z, size_x, stride=pitch), :] = ref[at : at + size_x, :]
            at = 4 * HALO * size_x
            vol_ref[pl.ds(z, size_x, stride=pitch), :] = ref[at : at + size_x, :]
    first_lane = lax.broadcasted_iota(jnp.int32, (8, ny), 1) == 0
    last_lane = lax.broadcasted_iota(jnp.int32, (8, ny), 1) == ny - 1

    x_index = lax.axis_index("sub") * nx - HALO
    x_count = lax.axis_size("sub") * nx
    z_row = lax.broadcasted_iota(jnp.int32, (pitch, ny), 0) + (lax.axis_index("curve") * nz - HALO)
    z_free = (z_row > 0) & (z_row < lax.axis_size("curve") * nz)
    y_free = lax.broadcasted_iota(jnp.int32, (pitch, ny), 1) > 0
    free = (z_free & y_free).astype(jnp.float32)
    row_index = lax.broadcasted_iota(jnp.int32, (pitch, ny), 0)
    for x in range(size_x):
        below = max(x - 1, 0) * pitch
        above = min(x, size_x - 2) * pitch
        e = jnp.maximum(vol_ref[below : below + pitch, :], vol_ref[above : above + pitch, :])
        e = jnp.where(row_index < size_z - 1, e, pltpu.roll(e, 1, 0))
        before = jnp.where(row_index == 0, e, pltpu.roll(e, 1, 0))
        e = jnp.maximum(e, before)
        e = jnp.maximum(e, pltpu.roll(e, 1, 1))
        here = x_index + x
        x_free = jnp.where((here > 0) & (here < x_count), 1.0, 0.0)
        keep_ref[x * pitch : (x + 1) * pitch, :] = jnp.where(e > 0, free * x_free, 0.0)
    for x in range(size_x - 1):
        rows = pl.ds(x * pitch, pitch)
        dev_ref[rows, :] = vol_ref[rows, :] * (1.0 - dev_ref[rows, :])

    def store_node(x, z, value):
        ahead = jnp.where(last_lane, 0.0, pltpu.roll(value, ny - 1, 1))
        both = value + pltpu.roll(ahead, 3, 0)
        field_ref[x, :, z * ny : (z + 1) * ny] = value
        high = both.astype(jnp.bfloat16).astype(jnp.float32)
        split_ref[x, :, z * ny : (z + 1) * ny] = jnp.concatenate([high, both - high], axis=0).astype(jnp.bfloat16)

    blank = jnp.zeros((5, ny), jnp.float32)
    for x in range(size_x):
        for z in range(size_z):
            if z < HALO:
                rows = clow_ref[pl.ds(z * size_x + x, 3, stride=HALO * size_x), :]
            elif z >= HALO + nz:
                rows = chigh_ref[pl.ds((z - HALO - nz) * size_x + x, 3, stride=HALO * size_x), :]
            elif x < HALO:
                rows = slow_ref[pl.ds(x * nz + z - HALO, 3, stride=HALO * nz), :]
            elif x >= HALO + nx:
                rows = shigh_ref[pl.ds((x - HALO - nx) * nz + z - HALO, 3, stride=HALO * nz), :]
            else:
                rows = load_ref[pl.ds((x - HALO) * nz + z - HALO, 3, stride=nx * nz), :]
            value = jnp.concatenate([rows, blank], axis=0) * keep_ref[pl.ds(x * pitch + z, 1), :]
            store_node(x, z, value)

    def save(out_ref):
        for x in range(nx):
            for z in range(nz):
                value = field_ref[x + HALO, 0:3, (z + HALO) * ny : (z + HALO + 1) * ny]
                out_ref[pl.ds(x * nz + z, 3, stride=nx * nz), :] = value

    save(w0_ref)
    kmat = k_ref[...]
    inverse = scale_ref[0:1, 0:1]
    component = (lax.broadcasted_iota(jnp.int32, (8, ny), 0) < 3).astype(jnp.float32) * inverse

    for k in range(1, ITERS + 1):
        sum_ref[...] = jnp.zeros_like(sum_ref)

        for i in range(k - 1, size_x - k):
            z = k - 1
            end = size_z - k
            side_low = side_high = None
            while z < end:
                cols = min(2, end - z)
                lanes = cols * ny
                parts = []
                for a in (0, 1):
                    for c in (0, 1):
                        parts.append(split_ref[i + a, :, (z + c) * ny : (z + c) * ny + lanes])
                rhs = jnp.concatenate(parts + parts, axis=0)
                forces = jnp.dot(kmat, rhs, preferred_element_type=jnp.float32)
                for j in range(cols):
                    here = z + j
                    vol = vol_ref[pl.ds(i * pitch + here, 1), :]
                    dev = dev_ref[pl.ds(i * pitch + here, 1), :]
                    g = []
                    for q in range(4):
                        f_vol = forces[8 * q : 8 * q + 8, j * ny : (j + 1) * ny]
                        f_dev = forces[32 + 8 * q : 40 + 8 * q, j * ny : (j + 1) * ny]
                        g.append(vol * f_vol + dev * f_dev)
                    if here >= k:
                        span = slice(here * ny, (here + 1) * ny)
                        total = sum_ref[:, span] + (g[0] + side_low)
                        sum_ref[:, span] = g[2] + side_high
                        behind = jnp.where(first_lane, 0.0, pltpu.roll(total, 1, 1))
                        total = total + pltpu.roll(behind, 5, 0)
                        old = field_ref[i, :, span]
                        keep = keep_ref[pl.ds(i * pitch + here, 1), :]
                        store_node(i, here, old - (component * keep) * (total + ground_spring * old))
                    side_low, side_high = g[1], g[3]
                z += cols
        save(w_refs[k])

    sums = [jnp.zeros((8, ny), jnp.float32) for _ in PAIRS]
    for r in range(3 * nx * nz // 8):
        w = [ref[8 * r : 8 * r + 8, :] for ref in w_refs]
        for n, (i, j) in enumerate(PAIRS):
            sums[n] = sums[n] + w[i] * w[j]
    lane = lax.broadcasted_iota(jnp.int32, (1, ny), 1)
    row = jnp.zeros((1, ny), jnp.float32)
    for n, value in enumerate(sums):
        row = jnp.where(lane == n, jnp.sum(value, axis=(0, 1), keepdims=True), row)
    gram_ref[...] = jnp.broadcast_to(row[None], gram_ref.shape)


def finish_kernel(gram_ref, scale_ref, w0_ref, w1_ref, w2_ref, w3_ref, solution_ref, residual_ref):
    total = jnp.sum(gram_ref[...], axis=0)
    lane = lax.broadcasted_iota(jnp.int32, total.shape, 1)
    gram = {}
    for n, (i, j) in enumerate(PAIRS):
        value = jnp.sum(jnp.where(lane == n, total, 0.0), axis=1, keepdims=True)
        gram[i, j] = gram[j, i] = value

    def inner(p, q):
        result = None
        for i, left in enumerate(p):
            for j, right in enumerate(q):
                if left is not None and right is not None:
                    term = left * right * gram[i, j]
                    result = term if result is None else result + term
        return result

    def axpy(p, scale, q):
        out = []
        for left, right in zip(p, q):
            if right is None:
                out.append(left)
            else:
                out.append(scale * right if left is None else left + scale * right)
        return out

    def image_of(p):
        out = []
        for i in range(ITERS + 1):
            here = p[i]
            before = p[i - 1] if i > 0 else None
            if here is None:
                out.append(None if before is None else -before)
            else:
                out.append(here if before is None else here - before)
        return out

    one = jnp.ones((1, 1), jnp.float32)
    solution = [None] * (ITERS + 1)
    residual = [one] + [None] * ITERS
    image = image_of(residual)
    norm_now = inner(residual, residual)
    step = norm_now / inner(residual, image)
    direction = residual
    carried = image
    for iteration in range(ITERS):
        solution = axpy(solution, step, direction)
        residual = axpy(residual, -step, carried)
        if iteration + 1 < ITERS:
            image = image_of(residual)
            norm_next = inner(residual, residual)
            curvature = inner(residual, image)
            ratio = norm_next / norm_now
            step = norm_next / (curvature - ratio * norm_next / step)
            direction = axpy(residual, ratio, direction)
            carried = axpy(image, ratio, carried)
            norm_now = norm_next
    inverse = scale_ref[0:1, 0:1]
    w_refs = (w0_ref, w1_ref, w2_ref, w3_ref)
    solution = [None if c is None else c * inverse for c in solution]
    for out_ref, coefs in ((solution_ref, solution), (residual_ref, residual)):
        value = None
        for c, ref in zip(coefs, w_refs):
            if c is not None:
                value = c * ref[...] if value is None else value + c * ref[...]
        out_ref[...] = value


def local(load, plastic, tile_material, moduli, k_vol, k_dev):
    nx, nz, ny = plastic.shape
    dims = (nx, nz, ny) + tile_material.shape
    tx, tz = tile_material.shape[:2]
    f32 = jnp.float32
    vmem = pl.BlockSpec(memory_space=pltpu.VMEM)
    smem = pl.BlockSpec(memory_space=pltpu.SMEM)
    shape = jax.ShapeDtypeStruct
    load = load.reshape(3 * nx * nz, ny)
    plastic = plastic.reshape(nx * nz, ny)
    size_x = nx + 2 * HALO
    size_z = nz + 2 * HALO
    pitch = round_up(size_z, 8)
    sub_rows = round_up(4 * HALO * nz + tz, 8)
    curve_rows = round_up((4 * HALO + 1) * size_x, 8)
    count = lax.axis_size("curve") * lax.axis_size("sub")

    sub_a, sub_b, modulus, k_both, scale = pl.pallas_call(
        functools.partial(sub_message_kernel, dims),
        out_shape=(
            shape((sub_rows, ny), f32), shape((sub_rows, ny), f32), shape((round_up(tx * tz, 8), ny), f32),
            shape((64, 128), jnp.bfloat16), shape((8, 128), f32),
        ),
        in_specs=[smem, smem, vmem, vmem, vmem, vmem],
        out_specs=(vmem,) * 5,
        name="sub_message",
    )(tile_material, moduli, load, plastic, k_vol, k_dev)
    sub_a = exchange(sub_a, "sub", 0)
    sub_b = exchange(sub_b, "sub", 1)
    curve_a, curve_b = pl.pallas_call(
        functools.partial(curve_message_kernel, dims),
        out_shape=(shape((curve_rows, ny), f32),) * 2,
        in_specs=[vmem] * 5,
        out_specs=(vmem,) * 2,
        scratch_shapes=[pltpu.VMEM((sub_rows, ny), f32)] * 2,
        name="curve_message",
    )(load, plastic, modulus, sub_a, sub_b)
    curve_a = exchange(curve_a, "curve", 0)
    curve_b = exchange(curve_b, "curve", 1)
    *basis, gram = pl.pallas_call(
        functools.partial(product_kernel, dims),
        out_shape=(shape((3 * nx * nz, ny), f32),) * (ITERS + 1) + (shape((count, 1, ny), f32),),
        in_specs=[vmem] * 9,
        out_specs=(vmem,) * (ITERS + 2),
        scratch_shapes=[
            pltpu.VMEM((sub_rows, ny), f32), pltpu.VMEM((sub_rows, ny), f32),
            pltpu.VMEM((curve_rows, ny), f32), pltpu.VMEM((curve_rows, ny), f32),
            pltpu.VMEM((size_x * pitch, ny), f32), pltpu.VMEM((size_x * pitch, ny), f32),
            pltpu.VMEM((size_x * pitch, ny), f32),
            pltpu.VMEM((size_x, 8, size_z * ny), f32),
            pltpu.VMEM((size_x, 16, size_z * ny), jnp.bfloat16),
            pltpu.VMEM((8, size_z * ny), f32),
        ],
        name="products",
    )(load, plastic, modulus, sub_a, sub_b, curve_a, curve_b, k_both, scale)
    gram = lax.all_to_all(gram, AXES, 0, 0)
    solution_out, residual_out = pl.pallas_call(
        finish_kernel,
        out_shape=(shape((3 * nx * nz, ny), f32),) * 2,
        in_specs=[vmem] * 6,
        out_specs=(vmem,) * 2,
        name="finish",
    )(gram, scale, *basis)
    return solution_out.reshape(3, nx, nz, ny), residual_out.reshape(3, nx, nz, ny)


def solution(mesh):
    in_specs = (
        P(None, "sub", "curve", None),
        P("sub", "curve", None),
        P("sub", "curve", None),
        P(),
        P(),
        P(),
    )
    out_specs = (P(None, "sub", "curve", None), P(None, "sub", "curve", None))
    return jax.shard_map(local, mesh=mesh, in_specs=in_specs, out_specs=out_specs, check_vma=False)
```

```python
import functools

import jax
import jax.numpy as jnp
from jax import lax
from jax.experimental import pallas as pl
from jax.experimental.pallas import tpu as pltpu
from jax.sharding import PartitionSpec as P

TILE = 8
MATERIALS = 4
ITERS = 3
HALO = ITERS

ground_spring = 0.5

AXES = ("curve", "sub")
PAIRS = ((0, 0), (0, 1), (0, 2), (0, 3), (1, 1), (1, 2), (1, 3), (2, 2), (2, 3))


def round_up(value, to):
    return -(-value // to) * to


def exchange(value, axis, first):
    count = lax.axis_size(axis)
    pairs = []
    for i in range(first, count - 1, 2):
        pairs += [(i, i + 1), (i + 1, i)]
    return lax.ppermute(value, axis, pairs)


def is_odd(axis):
    return lax.axis_index(axis) % 2 == 1


def curve_message_kernel(dims, tile_ref, moduli_ref, load_ref, plastic_ref, a_ref, b_ref, modulus_ref):
    nx, nz, ny, tx, tz, ty = dims
    odd = is_odd("curve")
    lane = lax.broadcasted_iota(jnp.int32, (1, ny), 1) // TILE
    for t in range(tx * tz):
        row = jnp.zeros((1, ny), jnp.float32)
        for y in range(ty):
            material = tile_ref[t // tz, t % tz, y]
            value = jnp.float32(0)
            for m in range(MATERIALS):
                value = jnp.where(material == m + 1, moduli_ref[m], value)
            row = jnp.where(lane == y, value, row)
        modulus_ref[t : t + 1, :] = row
    for out_ref, z_first, tile_z in (
        (a_ref, jnp.where(odd, 0, nz - HALO), jnp.where(odd, 0, tz - 1)),
        (b_ref, jnp.where(odd, nz - HALO, 0), jnp.where(odd, tz - 1, 0)),
    ):
        for f in range(4):
            for zl in range(HALO):
                z = z_first + zl
                at = (f * HALO + zl) * nx
                if f < 3:
                    out_ref[at : at + nx, :] = load_ref[pl.ds(f * nx * nz + z, nx, stride=nz), :]
                else:
                    out_ref[at : at + nx, :] = plastic_ref[pl.ds(z, nx, stride=nz), :]
        for t in range(tx):
            at = 4 * HALO * nx + t
            out_ref[at : at + 1, :] = modulus_ref[pl.ds(t * tz + tile_z, 1), :]


def setup_kernel(moduli_ref, kv_ref, kd_ref, _, k_ref, scale_ref):
    r32 = lax.broadcasted_iota(jnp.int32, (32, 24), 0)
    m32 = lax.broadcasted_iota(jnp.int32, (32, 24), 1)
    spread_rows = ((m32 == 6 * (r32 // 8) + r32 % 8) & (r32 % 8 < 6)).astype(jnp.bfloat16)
    m24 = lax.broadcasted_iota(jnp.int32, (24, 128), 0)
    n24 = lax.broadcasted_iota(jnp.int32, (24, 128), 1)
    target = (m24 == 6 * (n24 % 64 // 16) + n24 % 8) & (n24 % 8 < 6)
    first_cols = (target & (n24 < 64)).astype(jnp.bfloat16)
    second_cols = (target & (n24 >= 64)).astype(jnp.bfloat16)
    dot = functools.partial(jnp.dot, preferred_element_type=jnp.float32)
    for at, ref in ((0, kv_ref), (32, kd_ref)):
        k = ref[...]
        high = k.astype(jnp.bfloat16)
        low = (k - high.astype(jnp.float32)).astype(jnp.bfloat16)
        part = dot(dot(spread_rows, high).astype(jnp.bfloat16), first_cols)
        part = part + dot(dot(spread_rows, low).astype(jnp.bfloat16), second_cols)
        k_ref[at : at + 32, :] = part.astype(jnp.bfloat16)

    def size(k):
        top = jnp.max(jnp.abs(k), axis=(0, 1), keepdims=True)
        safe = jnp.where(top > 0, top, 1.0)
        return top * jnp.sqrt(jnp.sum((k / safe) ** 2, axis=(0, 1), keepdims=True) * (1.0 / 24))

    mean_modulus = jnp.float32(0)
    for m in range(MATERIALS):
        mean_modulus = mean_modulus + moduli_ref[m] * (1.0 / MATERIALS)
    theta = ground_spring + 6.4 * mean_modulus * (size(kv_ref[...]) + 0.85 * size(kd_ref[...]))
    scale_ref[...] = jnp.broadcast_to(1.0 / theta, (8, 128))


def pick(ref_a, ref_b, odd, low_ref, high_ref):
    a = ref_a[...]
    b = ref_b[...]
    low_ref[...] = jnp.where(odd, a, b)
    high_ref[...] = jnp.where(odd, b, a)


def sub_message_kernel(dims, load_ref, plastic_ref, modulus_ref, ra_ref, rb_ref, a_ref, b_ref, low_ref, high_ref):
    nx, nz, ny, tx, tz, ty = dims
    size_z = nz + 2 * HALO
    pick(ra_ref, rb_ref, is_odd("curve"), low_ref, high_ref)
    odd = is_odd("sub")
    for out_ref, x_first, tile_x in (
        (a_ref, jnp.where(odd, 0, nx - HALO), jnp.where(odd, 0, tx - 1)),
        (b_ref, jnp.where(odd, nx - HALO, 0), jnp.where(odd, tx - 1, 0)),
    ):
        for f in range(4):
            for xl in range(HALO):
                at = (f * HALO + xl) * size_z
                x = x_first + xl
                if f < 3:
                    own = load_ref[pl.ds(f * nx * nz + x * nz, nz), :]
                else:
                    own = plastic_ref[pl.ds(x * nz, nz), :]
                side = f * HALO * nx
                out_ref[at : at + HALO, :] = low_ref[pl.ds(side + x, HALO, stride=nx), :]
                out_ref[at + HALO : at + HALO + nz, :] = own
                out_ref[at + HALO + nz : at + size_z, :] = high_ref[pl.ds(side + x, HALO, stride=nx), :]
        at = 4 * HALO * size_z
        out_ref[at : at + 1, :] = low_ref[pl.ds(4 * HALO * nx + tile_x, 1), :]
        out_ref[at + 1 : at + 1 + tz, :] = modulus_ref[pl.ds(tile_x * tz, tz), :]
        out_ref[at + 1 + tz : at + 2 + tz, :] = high_ref[pl.ds(4 * HALO * nx + tile_x, 1), :]


def product_kernel(
    dims,
    load_ref, plastic_ref, modulus_ref, sa_ref, sb_ref, ca_ref, cb_ref, k_ref, scale_ref,
    w0_ref, w1_ref, w2_ref, w3_ref, gram_ref,
    slow_ref, shigh_ref, clow_ref, chigh_ref, vol_ref, dev_ref, keep_ref, field_ref, split_ref, sum_ref,
):
    nx, nz, ny, tx, tz, ty = dims
    size_x = nx + 2 * HALO
    size_z = nz + 2 * HALO
    pitch = round_up(size_z, 8)
    w_refs = (w0_ref, w1_ref, w2_ref, w3_ref)
    pick(sa_ref, sb_ref, is_odd("sub"), slow_ref, shigh_ref)
    pick(ca_ref, cb_ref, is_odd("curve"), clow_ref, chigh_ref)

    for x in range(size_x - 1):
        row = x * pitch
        if HALO <= x < HALO + nx:
            own = x - HALO
            dev_ref[row + HALO : row + HALO + nz, :] = plastic_ref[own * nz : (own + 1) * nz, :]
            e_ref, e_row = modulus_ref, own // TILE * tz
            rims = (clow_ref, 4 * HALO * nx + own // TILE), (chigh_ref, 4 * HALO * nx + own // TILE)
        else:
            side_ref, xl = (slow_ref, x) if x < HALO else (shigh_ref, x - HALO - nx)
            at = (3 * HALO + xl) * size_z
            dev_ref[row : row + size_z, :] = side_ref[at : at + size_z, :]
            at = 4 * HALO * size_z
            e_ref, e_row = side_ref, at + 1
            rims = (side_ref, at), (side_ref, at + 1 + tz)
        for t in range(tz):
            value = jnp.broadcast_to(e_ref[e_row + t : e_row + t + 1, :], (TILE, ny))
            first = row + HALO + t * TILE
            vol_ref[first : first + TILE, :] = value
        for (ref, at), first in zip(rims, (row, row + HALO + nz)):
            vol_ref[first : first + HALO, :] = jnp.broadcast_to(ref[at : at + 1, :], (HALO, ny))
    for zl in range(HALO):
        at = (3 * HALO + zl) * nx
        for ref, z in ((clow_ref, zl), (chigh_ref, HALO + nz + zl)):
            dev_ref[pl.ds(HALO * pitch + z, nx, stride=pitch), :] = ref[at : at + nx, :]
    first_lane = lax.broadcasted_iota(jnp.int32, (8, ny), 1) == 0
    last_lane = lax.broadcasted_iota(jnp.int32, (8, ny), 1) == ny - 1

    x_index = lax.axis_index("sub") * nx - HALO
    x_count = lax.axis_size("sub") * nx
    z_row = lax.broadcasted_iota(jnp.int32, (pitch, ny), 0) + (lax.axis_index("curve") * nz - HALO)
    z_free = (z_row > 0) & (z_row < lax.axis_size("curve") * nz)
    y_free = lax.broadcasted_iota(jnp.int32, (pitch, ny), 1) > 0
    free = (z_free & y_free).astype(jnp.float32)
    row_index = lax.broadcasted_iota(jnp.int32, (pitch, ny), 0)
    for x in range(size_x):
        below = max(x - 1, 0) * pitch
        above = min(x, size_x - 2) * pitch
        e = jnp.maximum(vol_ref[below : below + pitch, :], vol_ref[above : above + pitch, :])
        e = jnp.where(row_index < size_z - 1, e, pltpu.roll(e, 1, 0))
        before = jnp.where(row_index == 0, e, pltpu.roll(e, 1, 0))
        e = jnp.maximum(e, before)
        e = jnp.maximum(e, pltpu.roll(e, 1, 1))
        here = x_index + x
        x_free = jnp.where((here > 0) & (here < x_count), 1.0, 0.0)
        keep_ref[x * pitch : (x + 1) * pitch, :] = jnp.where(e > 0, free * x_free, 0.0)
    for x in range(size_x - 1):
        rows = pl.ds(x * pitch, pitch)
        dev_ref[rows, :] = vol_ref[rows, :] * (1.0 - dev_ref[rows, :])

    def store_node(x, z, value):
        ahead = jnp.where(last_lane, 0.0, pltpu.roll(value, ny - 1, 1))
        both = value + pltpu.roll(ahead, 3, 0)
        field_ref[x, :, z * ny : (z + 1) * ny] = value
        high = both.astype(jnp.bfloat16).astype(jnp.float32)
        split_ref[x, :, z * ny : (z + 1) * ny] = jnp.concatenate([high, both - high], axis=0).astype(jnp.bfloat16)

    blank = jnp.zeros((5, ny), jnp.float32)
    for x in range(size_x):
        for z in range(size_z):
            if x < HALO:
                rows = slow_ref[pl.ds(x * size_z + z, 3, stride=HALO * size_z), :]
            elif x >= HALO + nx:
                rows = shigh_ref[pl.ds((x - HALO - nx) * size_z + z, 3, stride=HALO * size_z), :]
            elif z < HALO:
                rows = clow_ref[pl.ds(z * nx + x - HALO, 3, stride=HALO * nx), :]
            elif z >= HALO + nz:
                rows = chigh_ref[pl.ds((z - HALO - nz) * nx + x - HALO, 3, stride=HALO * nx), :]
            else:
                rows = load_ref[pl.ds((x - HALO) * nz + z - HALO, 3, stride=nx * nz), :]
            value = jnp.concatenate([rows, blank], axis=0) * keep_ref[pl.ds(x * pitch + z, 1), :]
            store_node(x, z, value)

    def save(out_ref):
        for x in range(nx):
            for z in range(nz):
                value = field_ref[x + HALO, 0:3, (z + HALO) * ny : (z + HALO + 1) * ny]
                out_ref[pl.ds(x * nz + z, 3, stride=nx * nz), :] = value

    save(w0_ref)
    kmat = k_ref[...]
    inverse = scale_ref[0:1, 0:1]
    component = (lax.broadcasted_iota(jnp.int32, (8, ny), 0) < 3).astype(jnp.float32) * inverse

    for k in range(1, ITERS + 1):
        sum_ref[...] = jnp.zeros_like(sum_ref)

        for i in range(k - 1, size_x - k):
            z = k - 1
            end = size_z - k
            side_low = side_high = None
            while z < end:
                cols = min(2, end - z)
                lanes = cols * ny
                parts = []
                for a in (0, 1):
                    for c in (0, 1):
                        parts.append(split_ref[i + a, :, (z + c) * ny : (z + c) * ny + lanes])
                rhs = jnp.concatenate(parts + parts, axis=0)
                forces = jnp.dot(kmat, rhs, preferred_element_type=jnp.float32)
                for j in range(cols):
                    here = z + j
                    vol = vol_ref[pl.ds(i * pitch + here, 1), :]
                    dev = dev_ref[pl.ds(i * pitch + here, 1), :]
                    g = []
                    for q in range(4):
                        f_vol = forces[8 * q : 8 * q + 8, j * ny : (j + 1) * ny]
                        f_dev = forces[32 + 8 * q : 40 + 8 * q, j * ny : (j + 1) * ny]
                        g.append(vol * f_vol + dev * f_dev)
                    if here >= k:
                        span = slice(here * ny, (here + 1) * ny)
                        total = sum_ref[:, span] + (g[0] + side_low)
                        sum_ref[:, span] = g[2] + side_high
                        behind = jnp.where(first_lane, 0.0, pltpu.roll(total, 1, 1))
                        total = total + pltpu.roll(behind, 5, 0)
                        old = field_ref[i, :, span]
                        keep = keep_ref[pl.ds(i * pitch + here, 1), :]
                        store_node(i, here, old - (component * keep) * (total + ground_spring * old))
                    side_low, side_high = g[1], g[3]
                z += cols
        save(w_refs[k])

    sums = [jnp.zeros((8, ny), jnp.float32) for _ in PAIRS]
    for r in range(3 * nx * nz // 8):
        w = [ref[8 * r : 8 * r + 8, :] for ref in w_refs]
        for n, (i, j) in enumerate(PAIRS):
            sums[n] = sums[n] + w[i] * w[j]
    lane = lax.broadcasted_iota(jnp.int32, (1, ny), 1)
    row = jnp.zeros((1, ny), jnp.float32)
    for n, value in enumerate(sums):
        row = jnp.where(lane == n, jnp.sum(value, axis=(0, 1), keepdims=True), row)
    gram_ref[...] = jnp.broadcast_to(row[None], gram_ref.shape)


def finish_kernel(gram_ref, scale_ref, w0_ref, w1_ref, w2_ref, w3_ref, solution_ref, residual_ref):
    total = jnp.sum(gram_ref[...], axis=0)
    lane = lax.broadcasted_iota(jnp.int32, total.shape, 1)
    gram = {}
    for n, (i, j) in enumerate(PAIRS):
        value = jnp.sum(jnp.where(lane == n, total, 0.0), axis=1, keepdims=True)
        gram[i, j] = gram[j, i] = value

    def inner(p, q):
        result = None
        for i, left in enumerate(p):
            for j, right in enumerate(q):
                if left is not None and right is not None:
                    term = left * right * gram[i, j]
                    result = term if result is None else result + term
        return result

    def axpy(p, scale, q):
        out = []
        for left, right in zip(p, q):
            if right is None:
                out.append(left)
            else:
                out.append(scale * right if left is None else left + scale * right)
        return out

    def image_of(p):
        out = []
        for i in range(ITERS + 1):
            here = p[i]
            before = p[i - 1] if i > 0 else None
            if here is None:
                out.append(None if before is None else -before)
            else:
                out.append(here if before is None else here - before)
        return out

    one = jnp.ones((1, 1), jnp.float32)
    solution = [None] * (ITERS + 1)
    residual = [one] + [None] * ITERS
    image = image_of(residual)
    norm_now = inner(residual, residual)
    step = norm_now / inner(residual, image)
    direction = residual
    carried = image
    for iteration in range(ITERS):
        solution = axpy(solution, step, direction)
        residual = axpy(residual, -step, carried)
        if iteration + 1 < ITERS:
            image = image_of(residual)
            norm_next = inner(residual, residual)
            curvature = inner(residual, image)
            ratio = norm_next / norm_now
            step = norm_next / (curvature - ratio * norm_next / step)
            direction = axpy(residual, ratio, direction)
            carried = axpy(image, ratio, carried)
            norm_now = norm_next
    inverse = scale_ref[0:1, 0:1]
    w_refs = (w0_ref, w1_ref, w2_ref, w3_ref)
    solution = [None if c is None else c * inverse for c in solution]
    for out_ref, coefs in ((solution_ref, solution), (residual_ref, residual)):
        value = None
        for c, ref in zip(coefs, w_refs):
            if c is not None:
                value = c * ref[...] if value is None else value + c * ref[...]
        out_ref[...] = value


def local(load, plastic, tile_material, moduli, k_vol, k_dev):
    nx, nz, ny = plastic.shape
    dims = (nx, nz, ny) + tile_material.shape
    tx, tz = tile_material.shape[:2]
    f32 = jnp.float32
    vmem = pl.BlockSpec(memory_space=pltpu.VMEM)
    smem = pl.BlockSpec(memory_space=pltpu.SMEM)
    shape = jax.ShapeDtypeStruct
    kept = pltpu.VMEM

    def near(*values):
        return [pltpu.with_memory_space_constraint(v, pltpu.VMEM) for v in values]

    load = load.reshape(3 * nx * nz, ny)
    plastic = plastic.reshape(nx * nz, ny)
    size_x = nx + 2 * HALO
    size_z = nz + 2 * HALO
    pitch = round_up(size_z, 8)
    curve_rows = round_up(4 * HALO * nx + tx, 8)
    sub_rows = round_up(4 * HALO * size_z + tz + 2, 8)
    count = lax.axis_size("curve") * lax.axis_size("sub")

    curve_a, curve_b, modulus = pl.pallas_call(
        functools.partial(curve_message_kernel, dims),
        out_shape=(kept((curve_rows, ny), f32), kept((curve_rows, ny), f32), kept((round_up(tx * tz, 8), ny), f32)),
        in_specs=[smem, smem, vmem, vmem],
        out_specs=(vmem,) * 3,
        name="curve_message",
    )(tile_material, moduli, load, plastic)
    k_both, scale = pl.pallas_call(
        setup_kernel,
        out_shape=(kept((64, 128), jnp.bfloat16), kept((8, 128), f32)),
        in_specs=[smem, vmem, vmem, vmem],
        out_specs=(vmem,) * 2,
        name="setup",
    )(moduli, k_vol, k_dev, *near(modulus))
    curve_a = exchange(curve_a, "curve", 0)
    curve_b = exchange(curve_b, "curve", 1)
    sub_a, sub_b = pl.pallas_call(
        functools.partial(sub_message_kernel, dims),
        out_shape=(kept((sub_rows, ny), f32),) * 2,
        in_specs=[vmem] * 5,
        out_specs=(vmem,) * 2,
        scratch_shapes=[pltpu.VMEM((curve_rows, ny), f32)] * 2,
        name="sub_message",
    )(*near(load, plastic, modulus, curve_a, curve_b))
    sub_a = exchange(sub_a, "sub", 0)
    sub_b = exchange(sub_b, "sub", 1)
    *basis, gram = pl.pallas_call(
        functools.partial(product_kernel, dims),
        out_shape=(kept((3 * nx * nz, ny), f32),) * (ITERS + 1) + (kept((count, 1, ny), f32),),
        in_specs=[vmem] * 9,
        out_specs=(vmem,) * (ITERS + 2),
        scratch_shapes=[
            pltpu.VMEM((sub_rows, ny), f32), pltpu.VMEM((sub_rows, ny), f32),
            pltpu.VMEM((curve_rows, ny), f32), pltpu.VMEM((curve_rows, ny), f32),
            pltpu.VMEM((size_x * pitch, ny), f32), pltpu.VMEM((size_x * pitch, ny), f32),
            pltpu.VMEM((size_x * pitch, ny), f32),
            pltpu.VMEM((size_x, 8, size_z * ny), f32),
            pltpu.VMEM((size_x, 16, size_z * ny), jnp.bfloat16),
            pltpu.VMEM((8, size_z * ny), f32),
        ],
        name="products",
    )(*near(load, plastic, modulus, sub_a, sub_b, curve_a, curve_b, k_both, scale))
    gram = lax.all_to_all(gram, AXES, 0, 0)
    solution_out, residual_out = pl.pallas_call(
        finish_kernel,
        out_shape=(shape((3 * nx * nz, ny), f32),) * 2,
        in_specs=[vmem] * 6,
        out_specs=(vmem,) * 2,
        name="finish",
    )(*near(gram, scale, *basis))
    return solution_out.reshape(3, nx, nz, ny), residual_out.reshape(3, nx, nz, ny)


def solution(mesh):
    in_specs = (
        P(None, "sub", "curve", None),
        P("sub", "curve", None),
        P("sub", "curve", None),
        P(),
        P(),
        P(),
    )
    out_specs = (P(None, "sub", "curve", None), P(None, "sub", "curve", None))
    return jax.shard_map(local, mesh=mesh, in_specs=in_specs, out_specs=out_specs, check_vma=False)
```

```python
import functools

import jax
import jax.numpy as jnp
from jax import lax
from jax.experimental import pallas as pl
from jax.experimental.pallas import tpu as pltpu
from jax.sharding import PartitionSpec as P


TILE = 8
MATERIALS = 4
ITERS = 3
HALO = ITERS

ground_spring = 0.5

AXES = ("curve", "sub")
MAX_GROWTH = 40.0
PAIRS = ((0, 0), (0, 1), (0, 2), (0, 3), (1, 1), (1, 2), (1, 3), (2, 2), (2, 3), (3, 3))


def round_up(value, to):
    return -(-value // to) * to


def exchange(value, axis, first):
    count = lax.axis_size(axis)
    pairs = []
    for i in range(first, count - 1, 2):
        pairs += [(i, i + 1), (i + 1, i)]
    return lax.ppermute(value, axis, pairs)


def is_odd(axis):
    return lax.axis_index(axis) % 2 == 1


def curve_message_kernel(dims, tile_ref, moduli_ref, load_ref, plastic_ref, a_ref, b_ref, modulus_ref):
    nx, nz, ny, tx, tz, ty = dims
    odd = is_odd("curve")
    lane = lax.broadcasted_iota(jnp.int32, (1, ny), 1) // TILE
    for t in range(tx * tz):
        row = jnp.zeros((1, ny), jnp.float32)
        for y in range(ty):
            material = tile_ref[t // tz, t % tz, y]
            value = jnp.float32(0)
            for m in range(MATERIALS):
                value = jnp.where(material == m + 1, moduli_ref[m], value)
            row = jnp.where(lane == y, value, row)
        modulus_ref[t : t + 1, :] = row
    for out_ref, z_first, tile_z in (
        (a_ref, jnp.where(odd, 0, nz - HALO), jnp.where(odd, 0, tz - 1)),
        (b_ref, jnp.where(odd, nz - HALO, 0), jnp.where(odd, tz - 1, 0)),
    ):
        for f in range(4):
            for zl in range(HALO):
                z = z_first + zl
                at = (f * HALO + zl) * nx
                if f < 3:
                    out_ref[at : at + nx, :] = load_ref[pl.ds(f * nx * nz + z, nx, stride=nz), :]
                else:
                    out_ref[at : at + nx, :] = plastic_ref[pl.ds(z, nx, stride=nz), :]
        for t in range(tx):
            at = 4 * HALO * nx + t
            out_ref[at : at + 1, :] = modulus_ref[pl.ds(t * tz + tile_z, 1), :]


def setup_kernel(moduli_ref, kv_ref, kd_ref, _, k_ref, scale_ref):
    r32 = lax.broadcasted_iota(jnp.int32, (32, 24), 0)
    m32 = lax.broadcasted_iota(jnp.int32, (32, 24), 1)
    spread_rows = ((m32 == 6 * (r32 // 8) + r32 % 8) & (r32 % 8 < 6)).astype(jnp.bfloat16)
    m24 = lax.broadcasted_iota(jnp.int32, (24, 128), 0)
    n24 = lax.broadcasted_iota(jnp.int32, (24, 128), 1)
    target = (m24 == 6 * (n24 % 64 // 16) + n24 % 8) & (n24 % 8 < 6)
    first_cols = (target & (n24 < 64)).astype(jnp.bfloat16)
    second_cols = (target & (n24 >= 64)).astype(jnp.bfloat16)
    dot = functools.partial(jnp.dot, preferred_element_type=jnp.float32)
    for at, ref in ((0, kv_ref), (32, kd_ref)):
        k = ref[...]
        high = k.astype(jnp.bfloat16)
        low = (k - high.astype(jnp.float32)).astype(jnp.bfloat16)
        part = dot(dot(spread_rows, high).astype(jnp.bfloat16), first_cols)
        part = part + dot(dot(spread_rows, low).astype(jnp.bfloat16), second_cols)
        k_ref[at : at + 32, :] = part.astype(jnp.bfloat16)

    def size(k):
        top = jnp.max(jnp.abs(k), axis=(0, 1), keepdims=True)
        safe = jnp.where(top > 0, top, 1.0)
        return top * jnp.sqrt(jnp.sum((k / safe) ** 2, axis=(0, 1), keepdims=True) * (1.0 / 24))

    mean_modulus = jnp.float32(0)
    for m in range(MATERIALS):
        mean_modulus = mean_modulus + moduli_ref[m] * (1.0 / MATERIALS)
    theta = ground_spring + 6.6 * mean_modulus * (size(kv_ref[...]) + size(kd_ref[...]))
    scale_ref[...] = jnp.broadcast_to(1.0 / theta, (8, 128))


def pick(ref_a, ref_b, odd, low_ref, high_ref):
    a = ref_a[...]
    b = ref_b[...]
    low_ref[...] = jnp.where(odd, a, b)
    high_ref[...] = jnp.where(odd, b, a)


def sub_message_kernel(dims, load_ref, plastic_ref, modulus_ref, ra_ref, rb_ref, _, a_ref, b_ref, low_ref, high_ref):
    nx, nz, _, tx, tz, _ = dims
    size_z = nz + 2 * HALO
    pick(ra_ref, rb_ref, is_odd("curve"), low_ref, high_ref)
    odd = is_odd("sub")
    for out_ref, x_first, tile_x in (
        (a_ref, jnp.where(odd, 0, nx - HALO), jnp.where(odd, 0, tx - 1)),
        (b_ref, jnp.where(odd, nx - HALO, 0), jnp.where(odd, tx - 1, 0)),
    ):
        for f in range(4):
            for xl in range(HALO):
                at = (f * HALO + xl) * size_z
                x = x_first + xl
                if f < 3:
                    own = load_ref[pl.ds(f * nx * nz + x * nz, nz), :]
                else:
                    own = plastic_ref[pl.ds(x * nz, nz), :]
                side = f * HALO * nx
                out_ref[at : at + HALO, :] = low_ref[pl.ds(side + x, HALO, stride=nx), :]
                out_ref[at + HALO : at + HALO + nz, :] = own
                out_ref[at + HALO + nz : at + size_z, :] = high_ref[pl.ds(side + x, HALO, stride=nx), :]
        at = 4 * HALO * size_z
        out_ref[at : at + 1, :] = low_ref[pl.ds(4 * HALO * nx + tile_x, 1), :]
        out_ref[at + 1 : at + 1 + tz, :] = modulus_ref[pl.ds(tile_x * tz, tz), :]
        out_ref[at + 1 + tz : at + 2 + tz, :] = high_ref[pl.ds(4 * HALO * nx + tile_x, 1), :]


def product_kernel(
    dims,
    load_ref, plastic_ref, modulus_ref, sa_ref, sb_ref, ca_ref, cb_ref, k_ref, scale_ref,
    w0_ref, w1_ref, w2_ref, w3_ref, gram_ref,
    slow_ref, shigh_ref, clow_ref, chigh_ref, vol_ref, dev_ref, keep_ref, field_ref, split_ref, sum_ref,
):
    nx, nz, ny, _, tz, _ = dims
    size_x = nx + 2 * HALO
    size_z = nz + 2 * HALO
    pitch = round_up(size_z, 8)
    w_refs = (w0_ref, w1_ref, w2_ref, w3_ref)
    pick(sa_ref, sb_ref, is_odd("sub"), slow_ref, shigh_ref)
    pick(ca_ref, cb_ref, is_odd("curve"), clow_ref, chigh_ref)

    for x in range(size_x - 1):
        row = x * pitch
        if HALO <= x < HALO + nx:
            own = x - HALO
            dev_ref[row + HALO : row + HALO + nz, :] = plastic_ref[own * nz : (own + 1) * nz, :]
            e_ref, e_row = modulus_ref, own // TILE * tz
            rims = (clow_ref, 4 * HALO * nx + own // TILE), (chigh_ref, 4 * HALO * nx + own // TILE)
        else:
            side_ref, xl = (slow_ref, x) if x < HALO else (shigh_ref, x - HALO - nx)
            at = (3 * HALO + xl) * size_z
            dev_ref[row : row + size_z, :] = side_ref[at : at + size_z, :]
            at = 4 * HALO * size_z
            e_ref, e_row = side_ref, at + 1
            rims = (side_ref, at), (side_ref, at + 1 + tz)
        for t in range(tz):
            value = jnp.broadcast_to(e_ref[e_row + t : e_row + t + 1, :], (TILE, ny))
            first = row + HALO + t * TILE
            vol_ref[first : first + TILE, :] = value
        for (ref, at), first in zip(rims, (row, row + HALO + nz)):
            vol_ref[first : first + HALO, :] = jnp.broadcast_to(ref[at : at + 1, :], (HALO, ny))
    for zl in range(HALO):
        at = (3 * HALO + zl) * nx
        for ref, z in ((clow_ref, zl), (chigh_ref, HALO + nz + zl)):
            dev_ref[pl.ds(HALO * pitch + z, nx, stride=pitch), :] = ref[at : at + nx, :]
    first_lane = lax.broadcasted_iota(jnp.int32, (8, ny), 1) == 0
    last_lane = lax.broadcasted_iota(jnp.int32, (8, ny), 1) == ny - 1

    x_index = lax.axis_index("sub") * nx - HALO
    x_count = lax.axis_size("sub") * nx
    z_row = lax.broadcasted_iota(jnp.int32, (pitch, ny), 0) + (lax.axis_index("curve") * nz - HALO)
    z_free = (z_row > 0) & (z_row < lax.axis_size("curve") * nz)
    y_free = lax.broadcasted_iota(jnp.int32, (pitch, ny), 1) > 0
    free = (z_free & y_free).astype(jnp.float32)
    row_index = lax.broadcasted_iota(jnp.int32, (pitch, ny), 0)
    for x in range(size_x):
        below = max(x - 1, 0) * pitch
        above = min(x, size_x - 2) * pitch
        e = jnp.maximum(vol_ref[below : below + pitch, :], vol_ref[above : above + pitch, :])
        e = jnp.where(row_index < size_z - 1, e, pltpu.roll(e, 1, 0))
        before = jnp.where(row_index == 0, e, pltpu.roll(e, 1, 0))
        e = jnp.maximum(e, before)
        e = jnp.maximum(e, pltpu.roll(e, 1, 1))
        here = x_index + x
        x_free = jnp.where((here > 0) & (here < x_count), 1.0, 0.0)
        keep_ref[x * pitch : (x + 1) * pitch, :] = jnp.where(e > 0, free * x_free, 0.0)
    for x in range(size_x - 1):
        rows = pl.ds(x * pitch, pitch)
        dev_ref[rows, :] = vol_ref[rows, :] * (1.0 - dev_ref[rows, :])

    def store_node(x, z, value):
        ahead = jnp.where(last_lane, 0.0, pltpu.roll(value, ny - 1, 1))
        both = value + pltpu.roll(ahead, 3, 0)
        field_ref[x, :, z * ny : (z + 1) * ny] = value
        high = both.astype(jnp.bfloat16).astype(jnp.float32)
        split_ref[x, :, z * ny : (z + 1) * ny] = jnp.concatenate([high, both - high], axis=0).astype(jnp.bfloat16)

    blank = jnp.zeros((5, ny), jnp.float32)
    for x in range(size_x):
        for z in range(size_z):
            if x < HALO:
                rows = slow_ref[pl.ds(x * size_z + z, 3, stride=HALO * size_z), :]
            elif x >= HALO + nx:
                rows = shigh_ref[pl.ds((x - HALO - nx) * size_z + z, 3, stride=HALO * size_z), :]
            elif z < HALO:
                rows = clow_ref[pl.ds(z * nx + x - HALO, 3, stride=HALO * nx), :]
            elif z >= HALO + nz:
                rows = chigh_ref[pl.ds((z - HALO - nz) * nx + x - HALO, 3, stride=HALO * nx), :]
            else:
                rows = load_ref[pl.ds((x - HALO) * nz + z - HALO, 3, stride=nx * nz), :]
            value = jnp.concatenate([rows, blank], axis=0) * keep_ref[pl.ds(x * pitch + z, 1), :]
            store_node(x, z, value)

    def save(out_ref):
        for x in range(nx):
            for z in range(nz):
                value = field_ref[x + HALO, 0:3, (z + HALO) * ny : (z + HALO + 1) * ny]
                out_ref[pl.ds(x * nz + z, 3, stride=nx * nz), :] = value

    save(w0_ref)
    kmat = k_ref[...]
    inverse = scale_ref[0:1, 0:1]
    component = (lax.broadcasted_iota(jnp.int32, (8, ny), 0) < 3).astype(jnp.float32) * inverse

    for k in range(1, ITERS + 1):
        sum_ref[...] = jnp.zeros_like(sum_ref)

        for i in range(k - 1, size_x - k):
            z = k - 1
            end = size_z - k
            side_low = side_high = None
            while z < end:
                cols = min(2, end - z)
                lanes = cols * ny
                parts = []
                for a in (0, 1):
                    for c in (0, 1):
                        parts.append(split_ref[i + a, :, (z + c) * ny : (z + c) * ny + lanes])
                rhs = jnp.concatenate(parts + parts, axis=0)
                forces = jnp.dot(kmat, rhs, preferred_element_type=jnp.float32)
                for j in range(cols):
                    here = z + j
                    vol = vol_ref[pl.ds(i * pitch + here, 1), :]
                    dev = dev_ref[pl.ds(i * pitch + here, 1), :]
                    g = []
                    for q in range(4):
                        f_vol = forces[8 * q : 8 * q + 8, j * ny : (j + 1) * ny]
                        f_dev = forces[32 + 8 * q : 40 + 8 * q, j * ny : (j + 1) * ny]
                        g.append(vol * f_vol + dev * f_dev)
                    if here >= k:
                        span = slice(here * ny, (here + 1) * ny)
                        total = sum_ref[:, span] + (g[0] + side_low)
                        sum_ref[:, span] = g[2] + side_high
                        behind = jnp.where(first_lane, 0.0, pltpu.roll(total, 1, 1))
                        total = total + pltpu.roll(behind, 5, 0)
                        old = field_ref[i, :, span]
                        keep = keep_ref[pl.ds(i * pitch + here, 1), :]
                        store_node(i, here, old - (component * keep) * (total + ground_spring * old))
                    side_low, side_high = g[1], g[3]
                z += cols
        save(w_refs[k])

    sums = [jnp.zeros((8, ny), jnp.float32) for _ in PAIRS]
    for r in range(3 * nx * nz // 8):
        w = [ref[8 * r : 8 * r + 8, :] for ref in w_refs]
        for n, (i, j) in enumerate(PAIRS):
            sums[n] = sums[n] + w[i] * w[j]
    lane = lax.broadcasted_iota(jnp.int32, (1, ny), 1)
    row = jnp.zeros((1, ny), jnp.float32)
    for n, value in enumerate(sums):
        row = jnp.where(lane == n, jnp.sum(value, axis=(0, 1), keepdims=True), row)
    gram_ref[...] = jnp.broadcast_to(row[None], gram_ref.shape)


def finish_kernel(gram_ref, scale_ref, w0_ref, w1_ref, w2_ref, w3_ref, solution_ref, residual_ref, better_ref, poor_ref):
    total = jnp.sum(gram_ref[...], axis=0)
    lane = lax.broadcasted_iota(jnp.int32, total.shape, 1)
    gram = {}
    for n, (i, j) in enumerate(PAIRS):
        value = jnp.sum(jnp.where(lane == n, total, 0.0), axis=1, keepdims=True)
        gram[i, j] = gram[j, i] = value

    def inner(p, q):
        result = None
        for i, left in enumerate(p):
            for j, right in enumerate(q):
                if left is not None and right is not None:
                    term = left * right * gram[i, j]
                    result = term if result is None else result + term
        return result

    def axpy(p, scale, q):
        out = []
        for left, right in zip(p, q):
            if right is None:
                out.append(left)
            else:
                out.append(scale * right if left is None else left + scale * right)
        return out

    def image_of(p):
        out = []
        for i in range(ITERS + 1):
            here = p[i]
            before = p[i - 1] if i > 0 else None
            if here is None:
                out.append(None if before is None else -before)
            else:
                out.append(here if before is None else here - before)
        return out

    one = jnp.ones((1, 1), jnp.float32)
    solution = [None] * (ITERS + 1)
    residual = [one] + [None] * ITERS
    image = image_of(residual)
    norm_now = inner(residual, residual)
    step = first_step = norm_now / inner(residual, image)
    direction = residual
    carried = image
    for iteration in range(ITERS):
        solution = axpy(solution, step, direction)
        residual = axpy(residual, -step, carried)
        if iteration + 1 < ITERS:
            image = image_of(residual)
            norm_next = inner(residual, residual)
            curvature = inner(residual, image)
            ratio = norm_next / norm_now
            step = norm_next / (curvature - ratio * norm_next / step)
            direction = axpy(residual, ratio, direction)
            carried = axpy(image, ratio, carried)
            norm_now = norm_next
    inverse = scale_ref[0:1, 0:1]
    better_ref[...] = jnp.broadcast_to(first_step * inverse, better_ref.shape)
    w_refs = (w0_ref, w1_ref, w2_ref, w3_ref)
    solution = [None if c is None else c * inverse for c in solution]
    for out_ref, coefs in ((solution_ref, solution), (residual_ref, residual)):
        value = None
        for c, ref in zip(coefs, w_refs):
            if c is not None:
                value = c * ref[...] if value is None else value + c * ref[...]
        out_ref[...] = value
    terms = None
    for i, c in enumerate(residual):
        size = jnp.abs(c) * jnp.sqrt(gram[i, i])
        terms = size if terms is None else terms + size
    well = terms <= MAX_GROWTH * jnp.sqrt(inner(residual, residual))
    poor_ref[0, 0] = jnp.where(jnp.max(jnp.where(well, 0.0, 1.0)) > 0, 1, 0)


def local(load, plastic, tile_material, moduli, k_vol, k_dev):
    nx, nz, ny = plastic.shape
    dims = (nx, nz, ny) + tile_material.shape
    tx, tz = tile_material.shape[:2]
    f32 = jnp.float32
    vmem = pl.BlockSpec(memory_space=pltpu.VMEM)
    smem = pl.BlockSpec(memory_space=pltpu.SMEM)
    shape = jax.ShapeDtypeStruct
    kept = pltpu.VMEM

    def near(*values):
        return [pltpu.with_memory_space_constraint(v, pltpu.VMEM) for v in values]

    load = load.reshape(3 * nx * nz, ny)
    plastic = plastic.reshape(nx * nz, ny)
    size_x = nx + 2 * HALO
    size_z = nz + 2 * HALO
    pitch = round_up(size_z, 8)
    curve_rows = round_up(4 * HALO * nx + tx, 8)
    sub_rows = round_up(4 * HALO * size_z + tz + 2, 8)
    count = lax.axis_size("curve") * lax.axis_size("sub")

    curve_a, curve_b, modulus = pl.pallas_call(
        functools.partial(curve_message_kernel, dims),
        out_shape=(kept((curve_rows, ny), f32), kept((curve_rows, ny), f32), kept((round_up(tx * tz, 8), ny), f32)),
        in_specs=[smem, smem, vmem, vmem],
        out_specs=(vmem,) * 3,
        name="curve_message",
    )(tile_material, moduli, load, plastic)
    k_both, scale = pl.pallas_call(
        setup_kernel,
        out_shape=(kept((64, 128), jnp.bfloat16), kept((8, 128), f32)),
        in_specs=[smem, vmem, vmem, vmem],
        out_specs=(vmem,) * 2,
        name="setup",
    )(moduli, k_vol, k_dev, *near(modulus))
    curve_b = exchange(curve_b, "curve", 1)
    curve_a = exchange(curve_a, "curve", 0)
    sub_a, sub_b = pl.pallas_call(
        functools.partial(sub_message_kernel, dims),
        out_shape=(kept((sub_rows, ny), f32),) * 2,
        in_specs=[vmem] * 6,
        out_specs=(vmem,) * 2,
        scratch_shapes=[pltpu.VMEM((curve_rows, ny), f32)] * 2,
        name="sub_message",
    )(*near(load, plastic, modulus, curve_a, curve_b, scale))
    sub_b = exchange(sub_b, "sub", 1)
    sub_a = exchange(sub_a, "sub", 0)

    def solve(scale):
        *basis, gram = pl.pallas_call(
            functools.partial(product_kernel, dims),
            out_shape=(kept((3 * nx * nz, ny), f32),) * (ITERS + 1) + (kept((count, 1, ny), f32),),
            in_specs=[vmem] * 9,
            out_specs=(vmem,) * (ITERS + 2),
            scratch_shapes=[
                pltpu.VMEM((sub_rows, ny), f32), pltpu.VMEM((sub_rows, ny), f32),
                pltpu.VMEM((curve_rows, ny), f32), pltpu.VMEM((curve_rows, ny), f32),
                pltpu.VMEM((size_x * pitch, ny), f32), pltpu.VMEM((size_x * pitch, ny), f32),
                pltpu.VMEM((size_x * pitch, ny), f32),
                pltpu.VMEM((size_x, 8, size_z * ny), f32),
                pltpu.VMEM((size_x, 16, size_z * ny), jnp.bfloat16),
                pltpu.VMEM((8, size_z * ny), f32),
            ],
            name="products",
        )(*near(load, plastic, modulus, sub_a, sub_b, curve_a, curve_b, k_both, scale))
        gram = lax.all_to_all(gram, AXES, 0, 0)
        return pl.pallas_call(
            finish_kernel,
            out_shape=(shape((3 * nx * nz, ny), f32),) * 2 + (kept((8, 128), f32), pltpu.SMEM((1, 1), jnp.int32)),
            in_specs=[vmem] * 6,
            out_specs=(vmem, vmem, vmem, smem),
            name="finish",
        )(*near(gram, scale, *basis))

    *found, better, poor = solve(scale)
    found = lax.cond(poor[0, 0] > 0, lambda: tuple(solve(better)[:2]), lambda: tuple(found))
    return tuple(value.reshape(3, nx, nz, ny) for value in found)


def solution(mesh):
    in_specs = (
        P(None, "sub", "curve", None),
        P("sub", "curve", None),
        P("sub", "curve", None),
        P(),
        P(),
        P(),
    )
    out_specs = (P(None, "sub", "curve", None), P(None, "sub", "curve", None))

    return jax.shard_map(local, mesh=mesh, in_specs=in_specs, out_specs=out_specs, check_vma=False)
```

```python
import collections
import functools

import jax
import jax.numpy as jnp
from jax import lax
from jax.experimental import pallas as pl
from jax.experimental.pallas import tpu as pltpu
from jax.sharding import PartitionSpec as P


TILE = 8
MATERIALS = 4
ITERS = 3
HALO = ITERS

ground_spring = 0.5

AXES = ("curve", "sub")
MAX_GROWTH = 40.0
PAIRS = ((0, 0), (0, 1), (0, 2), (0, 3), (1, 1), (1, 2), (1, 3), (2, 2), (2, 3), (3, 3))


def round_up(value, to):
    return -(-value // to) * to


def exchange(value, axis, first):
    count = lax.axis_size(axis)
    pairs = []
    for i in range(first, count - 1, 2):
        pairs += [(i, i + 1), (i + 1, i)]
    return lax.ppermute(value, axis, pairs)


def is_odd(axis):
    return lax.axis_index(axis) % 2 == 1


def curve_message_kernel(dims, tile_ref, moduli_ref, load_ref, plastic_ref, a_ref, b_ref, modulus_ref):
    nx, nz, ny, tx, tz, ty = dims
    odd = is_odd("curve")
    lane = lax.broadcasted_iota(jnp.int32, (1, ny), 1) // TILE
    for t in range(tx * tz):
        row = jnp.zeros((1, ny), jnp.float32)
        for y in range(ty):
            material = tile_ref[t // tz, t % tz, y]
            value = jnp.float32(0)
            for m in range(MATERIALS):
                value = jnp.where(material == m + 1, moduli_ref[m], value)
            row = jnp.where(lane == y, value, row)
        modulus_ref[t : t + 1, :] = row
    for out_ref, z_first, tile_z in (
        (a_ref, jnp.where(odd, 0, nz - HALO), jnp.where(odd, 0, tz - 1)),
        (b_ref, jnp.where(odd, nz - HALO, 0), jnp.where(odd, tz - 1, 0)),
    ):
        for f in range(4):
            for zl in range(HALO):
                z = z_first + zl
                at = (f * HALO + zl) * nx
                if f < 3:
                    out_ref[at : at + nx, :] = load_ref[pl.ds(f * nx * nz + z, nx, stride=nz), :]
                else:
                    out_ref[at : at + nx, :] = plastic_ref[pl.ds(z, nx, stride=nz), :]
        for t in range(tx):
            at = 4 * HALO * nx + t
            out_ref[at : at + 1, :] = modulus_ref[pl.ds(t * tz + tile_z, 1), :]


def setup_kernel(moduli_ref, kv_ref, kd_ref, _, k_ref, scale_ref):
    r32 = lax.broadcasted_iota(jnp.int32, (32, 24), 0)
    m32 = lax.broadcasted_iota(jnp.int32, (32, 24), 1)
    spread_rows = ((m32 == 6 * (r32 // 8) + r32 % 8) & (r32 % 8 < 6)).astype(jnp.bfloat16)
    m24 = lax.broadcasted_iota(jnp.int32, (24, 128), 0)
    n24 = lax.broadcasted_iota(jnp.int32, (24, 128), 1)
    target = (m24 == 6 * (n24 % 64 // 16) + n24 % 8) & (n24 % 8 < 6)
    first_cols = (target & (n24 < 64)).astype(jnp.bfloat16)
    second_cols = (target & (n24 >= 64)).astype(jnp.bfloat16)
    dot = functools.partial(jnp.dot, preferred_element_type=jnp.float32)
    for at, ref in ((0, kv_ref), (32, kd_ref)):
        k = ref[...]
        high = k.astype(jnp.bfloat16)
        low = (k - high.astype(jnp.float32)).astype(jnp.bfloat16)
        part = dot(dot(spread_rows, high).astype(jnp.bfloat16), first_cols)
        part = part + dot(dot(spread_rows, low).astype(jnp.bfloat16), second_cols)
        k_ref[at : at + 32, :] = part.astype(jnp.bfloat16)

    def size(k):
        top = jnp.max(jnp.abs(k), axis=(0, 1), keepdims=True)
        safe = jnp.where(top > 0, top, 1.0)
        return top * jnp.sqrt(jnp.sum((k / safe) ** 2, axis=(0, 1), keepdims=True) * (1.0 / 24))

    mean_modulus = jnp.float32(0)
    for m in range(MATERIALS):
        mean_modulus = mean_modulus + moduli_ref[m] * (1.0 / MATERIALS)
    theta = ground_spring + 6.6 * mean_modulus * (size(kv_ref[...]) + size(kd_ref[...]))
    scale_ref[...] = jnp.broadcast_to(1.0 / theta, (8, 128))


def pick(ref_a, ref_b, odd, low_ref, high_ref):
    a = ref_a[...]
    b = ref_b[...]
    low_ref[...] = jnp.where(odd, a, b)
    high_ref[...] = jnp.where(odd, b, a)


def sub_message_kernel(dims, load_ref, plastic_ref, modulus_ref, ra_ref, rb_ref, _, a_ref, b_ref, low_ref, high_ref):
    nx, nz, _, tx, tz, _ = dims
    size_z = nz + 2 * HALO
    pick(ra_ref, rb_ref, is_odd("curve"), low_ref, high_ref)
    odd = is_odd("sub")
    for out_ref, x_first, tile_x in (
        (a_ref, jnp.where(odd, 0, nx - HALO), jnp.where(odd, 0, tx - 1)),
        (b_ref, jnp.where(odd, nx - HALO, 0), jnp.where(odd, tx - 1, 0)),
    ):
        for f in range(4):
            for xl in range(HALO):
                at = (f * HALO + xl) * size_z
                x = x_first + xl
                if f < 3:
                    own = load_ref[pl.ds(f * nx * nz + x * nz, nz), :]
                else:
                    own = plastic_ref[pl.ds(x * nz, nz), :]
                side = f * HALO * nx
                out_ref[at : at + HALO, :] = low_ref[pl.ds(side + x, HALO, stride=nx), :]
                out_ref[at + HALO : at + HALO + nz, :] = own
                out_ref[at + HALO + nz : at + size_z, :] = high_ref[pl.ds(side + x, HALO, stride=nx), :]
        at = 4 * HALO * size_z
        out_ref[at : at + 1, :] = low_ref[pl.ds(4 * HALO * nx + tile_x, 1), :]
        out_ref[at + 1 : at + 1 + tz, :] = modulus_ref[pl.ds(tile_x * tz, tz), :]
        out_ref[at + 1 + tz : at + 2 + tz, :] = high_ref[pl.ds(4 * HALO * nx + tile_x, 1), :]


def inner_rows(nx, level):
    return range(1, nx) if level == 0 else range(level + 1, nx - level)


class Products:

    def __init__(self, dims, kmat, scale_ref):
        self.nx, self.nz, self.ny = dims[:3]
        self.size_x = self.nx + 2 * HALO
        self.size_z = self.nz + 2 * HALO
        self.pitch = round_up(self.size_z, 8)
        self.kmat = kmat
        lane = lax.broadcasted_iota(jnp.int32, (8, self.ny), 1)
        self.first_lane = lane == 0
        self.last_lane = lane == self.ny - 1
        rows = lax.broadcasted_iota(jnp.int32, (8, self.ny), 0)
        self.component = (rows < 3).astype(jnp.float32) * scale_ref[0:1, 0:1]
        self.blank = jnp.zeros((5, self.ny), jnp.float32)

    def span(self, z):
        return slice(z * self.ny, (z + 1) * self.ny)

    def deviatoric(self, refs, x):
        rows = slice(x * self.pitch, (x + 1) * self.pitch)
        refs.dev[rows, :] = refs.vol[rows, :] * (1.0 - refs.dev[rows, :])

    def mark_kept(self, refs, layers, vol_at):
        pitch, shape = self.pitch, (self.pitch, self.ny)
        x_index = lax.axis_index("sub") * self.nx - HALO
        x_count = lax.axis_size("sub") * self.nx
        z_row = lax.broadcasted_iota(jnp.int32, shape, 0)
        z_index = z_row + (lax.axis_index("curve") * self.nz - HALO)
        y_free = lax.broadcasted_iota(jnp.int32, shape, 1) > 0
        free = (z_index > 0) & (z_index < lax.axis_size("curve") * self.nz) & y_free
        free = free.astype(jnp.float32)
        for x in layers:
            below = max(x - 1, 0)
            above = min(x, self.size_x - 2)
            e = jnp.maximum(
                vol_at(below)[below * pitch : (below + 1) * pitch, :],
                vol_at(above)[above * pitch : (above + 1) * pitch, :],
            )
            e = jnp.where(z_row < self.size_z - 1, e, pltpu.roll(e, 1, 0))
            e = jnp.maximum(e, jnp.where(z_row == 0, e, pltpu.roll(e, 1, 0)))
            e = jnp.maximum(e, pltpu.roll(e, 1, 1))
            here = x_index + x
            x_free = jnp.where((here > 0) & (here < x_count), 1.0, 0.0)
            refs.keep[x * pitch : (x + 1) * pitch, :] = jnp.where(e > 0, free * x_free, 0.0)

    def store_node(self, refs, x, z, value, w_ref):
        ny, span = self.ny, self.span(z)
        ahead = jnp.where(self.last_lane, 0.0, pltpu.roll(value, ny - 1, 1))
        both = value + pltpu.roll(ahead, 3, 0)
        refs.field[x, :, span] = value
        high = both.astype(jnp.bfloat16).astype(jnp.float32)
        refs.split[x, :, span] = jnp.concatenate([high, both - high], axis=0).astype(jnp.bfloat16)
        own_x, own_z = x - HALO, z - HALO
        if 0 <= own_x < self.nx and 0 <= own_z < self.nz:
            w_ref[pl.ds(own_x * self.nz + own_z, 3, stride=self.nx * self.nz), :] = value[0:3, :]

    def start_node(self, refs, x, z, rows, w_ref):
        keep = refs.keep[pl.ds(x * self.pitch + z, 1), :]
        self.store_node(refs, x, z, jnp.concatenate([rows, self.blank], axis=0) * keep, w_ref)

    def update_node(self, refs, held, x, z, total, w_ref):
        behind = jnp.where(self.first_lane, 0.0, pltpu.roll(total, 1, 1))
        total = total + pltpu.roll(behind, 5, 0)
        old = held.field[x, :, self.span(z)]
        keep = held.keep[pl.ds(x * self.pitch + z, 1), :]
        value = old - (self.component * keep) * (total + ground_spring * old)
        self.store_node(refs, x, z, value, w_ref)

    def sweep(self, level, layers, split_at, coefficients_at, carried, emit, carry_to):
        for x in layers:
            vol_ref, dev_ref = coefficients_at(x)
            z, end = level - 1, self.size_z - level
            side_low = side_high = None
            while z < end:
                cols = min(2, end - z)
                lanes = cols * self.ny
                parts = []
                for a in (0, 1):
                    source = split_at(x + a)
                    for c in (0, 1):
                        parts.append(source[x + a, :, (z + c) * self.ny : (z + c) * self.ny + lanes])
                rhs = jnp.concatenate(parts + parts, axis=0)
                forces = jnp.dot(self.kmat, rhs, preferred_element_type=jnp.float32)
                for j in range(cols):
                    here = z + j
                    vol = vol_ref[pl.ds(x * self.pitch + here, 1), :]
                    dev = dev_ref[pl.ds(x * self.pitch + here, 1), :]
                    g = []
                    for q in range(4):
                        f_vol = forces[8 * q : 8 * q + 8, self.span(j)]
                        f_dev = forces[32 + 8 * q : 40 + 8 * q, self.span(j)]
                        g.append(vol * f_vol + dev * f_dev)
                    if here >= level:
                        before = None if carried is None else carried[:, self.span(here)]
                        carry_to[:, self.span(here)] = g[2] + side_high
                        emit(x, here, g[0] + side_low, before)
                    side_low, side_high = g[1], g[3]
                z += cols
            carried = carry_to


Refs = collections.namedtuple("Refs", ("vol", "dev", "keep", "field", "split"))


def gram_tiles(nx, nz, here, w_at, sums):
    for c in range(3):
        for x in range(nx):
            for t in range(nz // 8):
                at = (c * nx + x) * nz + 8 * t
                w = {}
                for n, (i, j) in enumerate(PAIRS):
                    if here(j, x):
                        for level in (i, j):
                            if level not in w:
                                w[level] = w_at(level, x)[at : at + 8, :]
                        term = w[i] * w[j]
                        sums[n] = term if sums[n] is None else sums[n] + term
    return sums


def inner_product_kernel(
    dims,
    load_ref, plastic_ref, modulus_ref, ca_ref, cb_ref, k_ref, scale_ref,
    w0_ref, w1_ref, w2_ref, w3_ref, part_ref, stash_ref,
    vol_ref, dev_ref, keep_ref, field_ref, split_ref, clow_ref, chigh_ref,
    sum_ref,
):
    nx, nz, ny, _, tz, _ = dims
    work = Products(dims, k_ref[...], scale_ref)
    pitch = work.pitch
    refs = Refs(vol_ref, dev_ref, keep_ref, field_ref, split_ref)
    w_refs = (w0_ref, w1_ref, w2_ref, w3_ref)
    pick(ca_ref, cb_ref, is_odd("curve"), clow_ref, chigh_ref)
    for own in range(nx):
        row = (own + HALO) * pitch
        dev_ref[row + HALO : row + HALO + nz, :] = plastic_ref[own * nz : (own + 1) * nz, :]
        tile_x = own // TILE
        for t in range(tz):
            value = modulus_ref[tile_x * tz + t : tile_x * tz + t + 1, :]
            first = row + HALO + t * TILE
            vol_ref[first : first + TILE, :] = jnp.broadcast_to(value, (TILE, ny))
        at = 4 * HALO * nx + tile_x
        for ref, first in ((clow_ref, row), (chigh_ref, row + HALO + nz)):
            vol_ref[first : first + HALO, :] = jnp.broadcast_to(ref[at : at + 1, :], (HALO, ny))
    for zl in range(HALO):
        at = (3 * HALO + zl) * nx
        for ref, z in ((clow_ref, zl), (chigh_ref, HALO + nz + zl)):
            dev_ref[pl.ds(HALO * pitch + z, nx, stride=pitch), :] = ref[at : at + nx, :]
    first, last = HALO + 1, HALO + nx - 1
    work.mark_kept(refs, range(first, last + 1), lambda x: vol_ref)
    for own in range(nx):
        work.deviatoric(refs, own + HALO)
    for x in range(first, last + 1):
        own = x - HALO
        for z in range(work.size_z):
            if z < HALO:
                rows = clow_ref[pl.ds(z * nx + own, 3, stride=HALO * nx), :]
            elif z >= HALO + nz:
                rows = chigh_ref[pl.ds((z - HALO - nz) * nx + own, 3, stride=HALO * nx), :]
            else:
                rows = load_ref[pl.ds(own * nz + z - HALO, 3, stride=nx * nz), :]
            work.start_node(refs, x, z, rows, w0_ref)
    for level in range(1, ITERS + 1):
        layers = range(HALO + level, HALO + nx - level)
        low_ref, high_ref = stash_ref.at[2 * level - 2], stash_ref.at[2 * level - 1]

        def emit(x, z, total, before, level=level, low_ref=low_ref):
            if before is None:
                low_ref[:, work.span(z)] = total
            else:
                work.update_node(refs, refs, x, z, total + before, w_refs[level])

        work.sweep(
            level, layers[:-1], lambda x: split_ref, lambda x: (vol_ref, dev_ref), None, emit, sum_ref
        )
        carried = sum_ref if len(layers) > 1 else None
        work.sweep(
            level, layers[-1:], lambda x: split_ref, lambda x: (vol_ref, dev_ref), carried, emit, high_ref
        )
    sums = gram_tiles(
        nx, nz, lambda j, x: x in inner_rows(nx, j), lambda j, x: w_refs[j], [None] * len(PAIRS)
    )
    for n, value in enumerate(sums):
        part_ref[8 * n : 8 * n + 8, :] = jnp.zeros((8, ny), jnp.float32) if value is None else value


def outer_product_kernel(
    dims,
    modulus_ref, load_ref, sa_ref, sb_ref, k_ref, scale_ref,
    a0_ref, a1_ref, a2_ref, a3_ref, part_ref, stash_ref,
    ivol_ref, idev_ref, ikeep_ref, ifield_ref, isplit_ref, clow_ref, chigh_ref,
    b0_ref, b1_ref, b2_ref, b3_ref, gram_ref,
    slow_ref, shigh_ref, vol_ref, dev_ref, keep_ref, field_ref, split_ref, sum_ref,
):
    nx, nz, ny, _, tz, _ = dims
    work = Products(dims, k_ref[...], scale_ref)
    pitch, size_x, size_z = work.pitch, work.size_x, work.size_z
    refs = Refs(vol_ref, dev_ref, keep_ref, field_ref, split_ref)
    inner = Refs(ivol_ref, idev_ref, ikeep_ref, ifield_ref, isplit_ref)
    a_refs = (a0_ref, a1_ref, a2_ref, a3_ref)
    b_refs = (b0_ref, b1_ref, b2_ref, b3_ref)
    pick(sa_ref, sb_ref, is_odd("sub"), slow_ref, shigh_ref)
    own_layers = range(HALO, HALO + nx)
    for x in range(size_x - 1):
        if x in own_layers:
            continue
        row = x * pitch
        side_ref, xl = (slow_ref, x) if x < HALO else (shigh_ref, x - HALO - nx)
        at = (3 * HALO + xl) * size_z
        dev_ref[row : row + size_z, :] = side_ref[at : at + size_z, :]
        at = 4 * HALO * size_z
        for t in range(tz):
            first = row + HALO + t * TILE
            value = side_ref[at + 1 + t : at + 2 + t, :]
            vol_ref[first : first + TILE, :] = jnp.broadcast_to(value, (TILE, ny))
        for rim, first in ((at, row), (at + 1 + tz, row + HALO + nz)):
            vol_ref[first : first + HALO, :] = jnp.broadcast_to(side_ref[rim : rim + 1, :], (HALO, ny))
    started = range(HALO + 1, HALO + nx)
    rest = [x for x in range(size_x) if x not in started]
    work.mark_kept(refs, rest, lambda x: ivol_ref if x in own_layers else vol_ref)
    for x in range(size_x - 1):
        if x not in own_layers:
            work.deviatoric(refs, x)
    for x in rest:
        for z in range(size_z):
            if x < HALO:
                rows = slow_ref[pl.ds(x * size_z + z, 3, stride=HALO * size_z), :]
            elif x >= HALO + nx:
                rows = shigh_ref[pl.ds((x - HALO - nx) * size_z + z, 3, stride=HALO * size_z), :]
            elif z < HALO:
                rows = clow_ref[pl.ds(z * nx + x - HALO, 3, stride=HALO * nx), :]
            elif z >= HALO + nz:
                rows = chigh_ref[pl.ds((z - HALO - nz) * nx + x - HALO, 3, stride=HALO * nx), :]
            else:
                rows = load_ref[pl.ds((x - HALO) * nz + z - HALO, 3, stride=nx * nz), :]
            work.start_node(refs, x, z, rows, b0_ref)

    held = {x: inner if x in started else refs for x in range(size_x)}
    keeps = dict(held)

    def update(x, z, total, level):
        source = keeps[x]._replace(field=held[x].field)
        work.update_node(refs, source, x, z, total, b_refs[level])

    def coefficients_at(x):
        source = inner if x in own_layers else refs
        return source.vol, source.dev

    for level in range(1, ITERS + 1):
        done = []

        def emit(x, z, total, before, level=level, done=done):
            if before is not None:
                update(x, z, total + before, level)
                done.append(x)

        def split_at(x):
            return held[x].split

        edge = HALO + level
        work.sweep(level, range(level - 1, edge), split_at, coefficients_at, None, emit, sum_ref)
        low_ref, high_ref = stash_ref.at[2 * level - 2], stash_ref.at[2 * level - 1]
        for z in range(level, size_z - level):
            update(edge, z, sum_ref[:, work.span(z)] + low_ref[:, work.span(z)], level)
        done.append(edge)
        upper = range(HALO + nx - level, size_x - level)
        work.sweep(level, upper, split_at, coefficients_at, high_ref, emit, sum_ref)
        for x in set(done):
            held[x] = refs

    sums = [part_ref[8 * n : 8 * n + 8, :] for n in range(len(PAIRS))]
    sums = gram_tiles(
        nx, nz, lambda j, x: x not in inner_rows(nx, j),
        lambda j, x: (a_refs if x in inner_rows(nx, j) else b_refs)[j], sums,
    )
    lane = lax.broadcasted_iota(jnp.int32, (1, ny), 1)
    row = jnp.zeros((1, ny), jnp.float32)
    for n, value in enumerate(sums):
        row = jnp.where(lane == n, jnp.sum(value, axis=(0, 1), keepdims=True), row)
    gram_ref[...] = jnp.broadcast_to(row[None], gram_ref.shape)


def finish_kernel(dims, gram_ref, scale_ref, *refs):
    nx, nz = dims[:2]
    a_refs, b_refs = refs[: ITERS + 1], refs[ITERS + 1 : 2 * ITERS + 2]
    solution_ref, residual_ref, better_ref, poor_ref = refs[2 * ITERS + 2 :]
    total = jnp.sum(gram_ref[...], axis=0)
    lane = lax.broadcasted_iota(jnp.int32, total.shape, 1)
    gram = {}
    for n, (i, j) in enumerate(PAIRS):
        value = jnp.sum(jnp.where(lane == n, total, 0.0), axis=1, keepdims=True)
        gram[i, j] = gram[j, i] = value

    def inner(p, q):
        result = None
        for i, left in enumerate(p):
            for j, right in enumerate(q):
                if left is not None and right is not None:
                    term = left * right * gram[i, j]
                    result = term if result is None else result + term
        return result

    def axpy(p, scale, q):
        out = []
        for left, right in zip(p, q):
            if right is None:
                out.append(left)
            else:
                out.append(scale * right if left is None else left + scale * right)
        return out

    def image_of(p):
        out = []
        for i in range(ITERS + 1):
            here = p[i]
            before = p[i - 1] if i > 0 else None
            if here is None:
                out.append(None if before is None else -before)
            else:
                out.append(here if before is None else here - before)
        return out

    one = jnp.ones((1, 1), jnp.float32)
    solution = [None] * (ITERS + 1)
    residual = [one] + [None] * ITERS
    image = image_of(residual)
    norm_now = inner(residual, residual)
    step = first_step = norm_now / inner(residual, image)
    direction = residual
    carried = image
    for iteration in range(ITERS):
        solution = axpy(solution, step, direction)
        residual = axpy(residual, -step, carried)
        if iteration + 1 < ITERS:
            image = image_of(residual)
            norm_next = inner(residual, residual)
            curvature = inner(residual, image)
            ratio = norm_next / norm_now
            step = norm_next / (curvature - ratio * norm_next / step)
            direction = axpy(residual, ratio, direction)
            carried = axpy(image, ratio, carried)
            norm_now = norm_next
    inverse = scale_ref[0:1, 0:1]
    better_ref[...] = jnp.broadcast_to(first_step * inverse, better_ref.shape)
    solution = [None if c is None else c * inverse for c in solution]
    for x in range(nx):
        for component in range(3):
            rows = slice((component * nx + x) * nz, (component * nx + x + 1) * nz)
            w = [(a_refs if x in inner_rows(nx, j) else b_refs)[j][rows, :] for j in range(ITERS + 1)]
            for out_ref, coefs in ((solution_ref, solution), (residual_ref, residual)):
                value = None
                for c, vector in zip(coefs, w):
                    if c is not None:
                        value = c * vector if value is None else value + c * vector
                out_ref[rows, :] = value
    terms = None
    for i, c in enumerate(residual):
        size = jnp.abs(c) * jnp.sqrt(gram[i, i])
        terms = size if terms is None else terms + size
    well = terms <= MAX_GROWTH * jnp.sqrt(inner(residual, residual))
    poor_ref[0, 0] = jnp.where(jnp.max(jnp.where(well, 0.0, 1.0)) > 0, 1, 0)


def local(load, plastic, tile_material, moduli, k_vol, k_dev):
    nx, nz, ny = plastic.shape
    dims = (nx, nz, ny) + tile_material.shape
    tx, tz = tile_material.shape[:2]
    f32 = jnp.float32
    vmem = pl.BlockSpec(memory_space=pltpu.VMEM)
    smem = pl.BlockSpec(memory_space=pltpu.SMEM)
    shape = jax.ShapeDtypeStruct
    kept = pltpu.VMEM
    grant = pltpu.CompilerParams(vmem_limit_bytes=16 * 2**20)

    def near(*values):
        return [pltpu.with_memory_space_constraint(v, pltpu.VMEM) for v in values]

    def far(*values):
        return [pltpu.with_memory_space_constraint(v, pltpu.HBM) for v in values]

    load = load.reshape(3 * nx * nz, ny)
    plastic = plastic.reshape(nx * nz, ny)
    size_x = nx + 2 * HALO
    size_z = nz + 2 * HALO
    pitch = round_up(size_z, 8)
    curve_rows = round_up(4 * HALO * nx + tx, 8)
    sub_rows = round_up(4 * HALO * size_z + tz + 2, 8)
    count = lax.axis_size("curve") * lax.axis_size("sub")

    curve_a, curve_b, modulus = pl.pallas_call(
        functools.partial(curve_message_kernel, dims),
        out_shape=(kept((curve_rows, ny), f32), kept((curve_rows, ny), f32), kept((round_up(tx * tz, 8), ny), f32)),
        in_specs=[smem, smem, vmem, vmem],
        out_specs=(vmem,) * 3,
        compiler_params=grant,
        name="curve_message",
    )(*far(tile_material, moduli, load, plastic))
    k_both, scale = pl.pallas_call(
        setup_kernel,
        out_shape=(kept((64, 128), jnp.bfloat16), kept((8, 128), f32)),
        in_specs=[smem, vmem, vmem, vmem],
        out_specs=(vmem,) * 2,
        compiler_params=grant,
        name="setup",
    )(*far(moduli), k_vol, k_dev, *near(modulus))
    curve_b = exchange(curve_b, "curve", 1)
    curve_a = exchange(curve_a, "curve", 0)
    sub_a, sub_b = pl.pallas_call(
        functools.partial(sub_message_kernel, dims),
        out_shape=(kept((sub_rows, ny), f32),) * 2,
        in_specs=[vmem] * 6,
        out_specs=(vmem,) * 2,
        scratch_shapes=[pltpu.VMEM((curve_rows, ny), f32)] * 2,
        compiler_params=grant,
        name="sub_message",
    )(*near(load, plastic, modulus, curve_a, curve_b, scale))
    sub_b = exchange(sub_b, "sub", 1)
    sub_a = exchange(sub_a, "sub", 0)
    basis_shape = (kept((3 * nx * nz, ny), f32),) * (ITERS + 1)
    coefficient = (size_x * pitch, ny)
    field = (size_x, 8, size_z * ny)
    split = (size_x, 16, size_z * ny)
    stash = (2 * ITERS, 8, size_z * ny)

    def solve(scale):
        *first, part, stashed, vol, dev, keep, fields, splits, low, high = pl.pallas_call(
            functools.partial(inner_product_kernel, dims),
            out_shape=basis_shape + (
                kept((8 * len(PAIRS), ny), f32), kept(stash, f32),
                kept(coefficient, f32), kept(coefficient, f32), kept(coefficient, f32),
                kept(field, f32), kept(split, jnp.bfloat16),
                kept((curve_rows, ny), f32), kept((curve_rows, ny), f32),
            ),
            in_specs=[vmem] * 7,
            out_specs=(vmem,) * (ITERS + 10),
            scratch_shapes=[pltpu.VMEM((8, size_z * ny), f32)],
            compiler_params=grant,
            name="inner_products",
        )(*near(load, plastic, modulus, curve_a, curve_b, k_both, scale))
        *second, gram = pl.pallas_call(
            functools.partial(outer_product_kernel, dims),
            out_shape=basis_shape + (kept((count, 1, ny), f32),),
            in_specs=[vmem] * (ITERS + 16),
            out_specs=(vmem,) * (ITERS + 2),
            scratch_shapes=[
                pltpu.VMEM((sub_rows, ny), f32), pltpu.VMEM((sub_rows, ny), f32),
                pltpu.VMEM(coefficient, f32), pltpu.VMEM(coefficient, f32), pltpu.VMEM(coefficient, f32),
                pltpu.VMEM(field, f32), pltpu.VMEM(split, jnp.bfloat16),
                pltpu.VMEM((8, size_z * ny), f32),
            ],
            compiler_params=grant,
            name="outer_products",
        )(*near(
            modulus, load, sub_a, sub_b, k_both, scale,
            *first, part, stashed, vol, dev, keep, fields, splits, low, high,
        ))
        gram = lax.all_to_all(gram, AXES, 0, 0)
        return pl.pallas_call(
            functools.partial(finish_kernel, dims),
            out_shape=(shape((3 * nx * nz, ny), f32),) * 2 + (kept((8, 128), f32), pltpu.SMEM((1, 1), jnp.int32)),
            in_specs=[vmem] * (2 * ITERS + 4),
            out_specs=(vmem, vmem, vmem, smem),
            compiler_params=grant,
            name="finish",
        )(*near(gram, scale, *first, *second))

    *found, better, poor = solve(scale)
    found = lax.cond(poor[0, 0] > 0, lambda: tuple(solve(better)[:2]), lambda: tuple(found))
    return tuple(value.reshape(3, nx, nz, ny) for value in found)


def solution(mesh):
    in_specs = (
        P(None, "sub", "curve", None),
        P("sub", "curve", None),
        P("sub", "curve", None),
        P(),
        P(),
        P(),
    )
    out_specs = (P(None, "sub", "curve", None), P(None, "sub", "curve", None))

    return jax.shard_map(local, mesh=mesh, in_specs=in_specs, out_specs=out_specs, check_vma=False)
```

```python
import collections
import functools

import jax
import jax.numpy as jnp
from jax import lax
from jax.experimental import pallas as pl
from jax.experimental.pallas import tpu as pltpu
from jax.sharding import PartitionSpec as P


TILE = 8
MATERIALS = 4
ITERS = 3
HALO = ITERS

ground_spring = 0.5

AXES = ("curve", "sub")
MAX_GROWTH = 40.0
PAIRS = ((0, 0), (0, 1), (0, 2), (0, 3), (1, 1), (1, 2), (1, 3), (2, 2), (2, 3), (3, 3))


def round_up(value, to):
    return -(-value // to) * to


def exchange(value, axis, first):
    count = lax.axis_size(axis)
    pairs = []
    for i in range(first, count - 1, 2):
        pairs += [(i, i + 1), (i + 1, i)]
    return lax.ppermute(value, axis, pairs)


def is_odd(axis):
    return lax.axis_index(axis) % 2 == 1


def curve_message_kernel(dims, tile_ref, moduli_ref, load_ref, plastic_ref, a_ref, b_ref, modulus_ref):
    nx, nz, ny, tx, tz, ty = dims
    odd = is_odd("curve")
    lane = lax.broadcasted_iota(jnp.int32, (1, ny), 1) // TILE
    for t in range(tx * tz):
        row = jnp.zeros((1, ny), jnp.float32)
        for y in range(ty):
            material = tile_ref[t // tz, t % tz, y]
            value = jnp.float32(0)
            for m in range(MATERIALS):
                value = jnp.where(material == m + 1, moduli_ref[m], value)
            row = jnp.where(lane == y, value, row)
        modulus_ref[t : t + 1, :] = row
    for out_ref, z_first, tile_z in (
        (a_ref, jnp.where(odd, 0, nz - HALO), jnp.where(odd, 0, tz - 1)),
        (b_ref, jnp.where(odd, nz - HALO, 0), jnp.where(odd, tz - 1, 0)),
    ):
        for f in range(4):
            for zl in range(HALO):
                z = z_first + zl
                at = (f * HALO + zl) * nx
                if f < 3:
                    out_ref[at : at + nx, :] = load_ref[pl.ds(f * nx * nz + z, nx, stride=nz), :]
                else:
                    out_ref[at : at + nx, :] = plastic_ref[pl.ds(z, nx, stride=nz), :]
        for t in range(tx):
            at = 4 * HALO * nx + t
            out_ref[at : at + 1, :] = modulus_ref[pl.ds(t * tz + tile_z, 1), :]


def setup_kernel(moduli_ref, kv_ref, kd_ref, _, k_ref, scale_ref):
    r32 = lax.broadcasted_iota(jnp.int32, (32, 24), 0)
    m32 = lax.broadcasted_iota(jnp.int32, (32, 24), 1)
    spread_rows = ((m32 == 6 * (r32 // 8) + r32 % 8) & (r32 % 8 < 6)).astype(jnp.bfloat16)
    m24 = lax.broadcasted_iota(jnp.int32, (24, 128), 0)
    n24 = lax.broadcasted_iota(jnp.int32, (24, 128), 1)
    target = (m24 == 6 * (n24 % 64 // 16) + n24 % 8) & (n24 % 8 < 6)
    first_cols = (target & (n24 < 64)).astype(jnp.bfloat16)
    second_cols = (target & (n24 >= 64)).astype(jnp.bfloat16)
    dot = functools.partial(jnp.dot, preferred_element_type=jnp.float32)
    for at, ref in ((0, kv_ref), (32, kd_ref)):
        k = ref[...]
        high = k.astype(jnp.bfloat16)
        low = (k - high.astype(jnp.float32)).astype(jnp.bfloat16)
        part = dot(dot(spread_rows, high).astype(jnp.bfloat16), first_cols)
        part = part + dot(dot(spread_rows, low).astype(jnp.bfloat16), second_cols)
        k_ref[at : at + 32, :] = part.astype(jnp.bfloat16)

    def size(k):
        top = jnp.max(jnp.abs(k), axis=(0, 1), keepdims=True)
        safe = jnp.where(top > 0, top, 1.0)
        return top * jnp.sqrt(jnp.sum((k / safe) ** 2, axis=(0, 1), keepdims=True) * (1.0 / 24))

    mean_modulus = jnp.float32(0)
    for m in range(MATERIALS):
        mean_modulus = mean_modulus + moduli_ref[m] * (1.0 / MATERIALS)
    theta = ground_spring + 6.6 * mean_modulus * (size(kv_ref[...]) + size(kd_ref[...]))
    scale_ref[...] = jnp.broadcast_to(1.0 / theta, (8, 128))


def pick(ref_a, ref_b, odd, low_ref, high_ref):
    a = ref_a[...]
    b = ref_b[...]
    low_ref[...] = jnp.where(odd, a, b)
    high_ref[...] = jnp.where(odd, b, a)


def sub_message_kernel(dims, load_ref, plastic_ref, modulus_ref, ra_ref, rb_ref, _, a_ref, b_ref, low_ref, high_ref):
    nx, nz, _, tx, tz, _ = dims
    size_z = nz + 2 * HALO
    pick(ra_ref, rb_ref, is_odd("curve"), low_ref, high_ref)
    odd = is_odd("sub")
    for out_ref, x_first, tile_x in (
        (a_ref, jnp.where(odd, 0, nx - HALO), jnp.where(odd, 0, tx - 1)),
        (b_ref, jnp.where(odd, nx - HALO, 0), jnp.where(odd, tx - 1, 0)),
    ):
        for f in range(4):
            for xl in range(HALO):
                at = (f * HALO + xl) * size_z
                x = x_first + xl
                if f < 3:
                    own = load_ref[pl.ds(f * nx * nz + x * nz, nz), :]
                else:
                    own = plastic_ref[pl.ds(x * nz, nz), :]
                side = f * HALO * nx
                out_ref[at : at + HALO, :] = low_ref[pl.ds(side + x, HALO, stride=nx), :]
                out_ref[at + HALO : at + HALO + nz, :] = own
                out_ref[at + HALO + nz : at + size_z, :] = high_ref[pl.ds(side + x, HALO, stride=nx), :]
        at = 4 * HALO * size_z
        out_ref[at : at + 1, :] = low_ref[pl.ds(4 * HALO * nx + tile_x, 1), :]
        out_ref[at + 1 : at + 1 + tz, :] = modulus_ref[pl.ds(tile_x * tz, tz), :]
        out_ref[at + 1 + tz : at + 2 + tz, :] = high_ref[pl.ds(4 * HALO * nx + tile_x, 1), :]


def inner_rows(nx, level):
    return range(1, nx) if level == 0 else range(level + 1, nx - level)


class Products:

    def __init__(self, dims, kmat, scale_ref):
        self.nx, self.nz, self.ny = dims[:3]
        self.size_x = self.nx + 2 * HALO
        self.size_z = self.nz + 2 * HALO
        self.pitch = round_up(self.size_z, 8)
        self.kmat = kmat
        self.component = lax.broadcasted_iota(jnp.int32, (8, self.ny), 0) < 3
        self.inverse = scale_ref[0:1, 0:1]
        self.blank = jnp.zeros((5, self.ny), jnp.float32)

    def span(self, z):
        return slice(z * self.ny, (z + 1) * self.ny)

    def tile(self, index):
        return (index // TILE + 1)

    def tile_row(self, x, z):
        return self.tile(x - HALO) * (self.nz // TILE + 2) + self.tile(z - HALO)

    def node_class(self, index):
        return self.tile(index - HALO - 1), self.tile(index - HALO)

    def mark_kept(self, refs, layers):
        self.rows = {}
        rows = refs.tiles.shape[0]
        lane = lax.broadcasted_iota(jnp.int32, (1, self.ny), 1)
        own, ahead = [], []
        for at in range(0, rows, 8):
            e = refs.tiles[at : at + 8, :]
            own.append(jnp.maximum(e, pltpu.roll(e, 1, 1)))
            ahead.append(jnp.maximum(e, pltpu.roll(e, self.ny - 1, 1)))
        own = jnp.concatenate(own, axis=0)
        ahead = jnp.concatenate(ahead, axis=0)
        per_x = self.nz // TILE + 2
        x_index = lax.axis_index("sub") * self.nx - HALO
        x_count = lax.axis_size("sub") * self.nx
        z_index = lax.axis_index("curve") * self.nz - HALO
        z_count = lax.axis_size("curve") * self.nz
        for x in layers:
            for z in range(self.size_z):
                key = self.node_class(x), self.node_class(z)
                if key in self.rows:
                    continue
                n = self.rows[key] = len(self.rows)
                free = (x_index + x > 0) & (x_index + x < x_count) & (z_index + z > 0) & (z_index + z < z_count)
                free = jnp.where(free, 1.0, 0.0)
                around = sorted({tx * per_x + tz for tx in key[0] for tz in key[1]})
                kept = []
                for e, inside in ((own, lane > 0), (ahead, lane < self.ny - 1)):
                    top = functools.reduce(jnp.maximum, [e[r : r + 1, :] for r in around])
                    kept.append(jnp.where(inside & (top > 0), free, 0.0))
                refs.keep[n : n + 1, :] = kept[0]
                refs.gain[n : n + 1, :] = kept[0] * self.inverse
                refs.ahead[n : n + 1, :] = kept[1] * self.inverse

    def kept_row(self, ref, x, z):
        n = self.rows[self.node_class(x), self.node_class(z)]
        return ref[n : n + 1, :]

    def store_node(self, refs, x, z, both, w_ref):
        span = self.span(z)
        refs.field[x, :, span] = both
        high = both.astype(jnp.bfloat16).astype(jnp.float32)
        refs.split[x, :, span] = jnp.concatenate([high, both - high], axis=0).astype(jnp.bfloat16)
        own_x, own_z = x - HALO, z - HALO
        if 0 <= own_x < self.nx and 0 <= own_z < self.nz:
            w_ref[pl.ds(own_x * self.nz + own_z, 3, stride=self.nx * self.nz), :] = both[0:3, :]

    def start_node(self, refs, x, z, rows, w_ref):
        value = jnp.concatenate([rows, self.blank], axis=0) * self.kept_row(refs.keep, x, z)
        ahead = pltpu.roll(pltpu.roll(value, self.ny - 1, 1), 3, 0)
        self.store_node(refs, x, z, value + ahead, w_ref)

    def update_node(self, refs, held, x, z, total, w_ref):
        below = pltpu.roll(pltpu.roll(total, 1, 1), 5, 0)
        above = pltpu.roll(pltpu.roll(total, self.ny - 1, 1), 3, 0)
        total = total + jnp.where(self.component, below, above)
        old = held.field[x, :, self.span(z)]
        gain = jnp.where(self.component, self.kept_row(refs.gain, x, z), self.kept_row(refs.ahead, x, z))
        self.store_node(refs, x, z, old - gain * (total + ground_spring * old), w_ref)

    def sweep(self, level, layers, split_at, coefficients_at, carried, emit, carry_to):
        for x in layers:
            tiles_ref, dev_ref = coefficients_at(x)
            z, end = level - 1, self.size_z - level
            side_low = side_high = None
            while z < end:
                cols = min(2, end - z)
                lanes = cols * self.ny
                parts = []
                for a in (0, 1):
                    source = split_at(x + a)
                    for c in (0, 1):
                        parts.append(source[x + a, :, (z + c) * self.ny : (z + c) * self.ny + lanes])
                rhs = jnp.concatenate(parts + parts, axis=0)
                forces = jnp.dot(self.kmat, rhs, preferred_element_type=jnp.float32)
                for j in range(cols):
                    here = z + j
                    row = self.tile_row(x, here)
                    vol = tiles_ref[row : row + 1, :]
                    dev = dev_ref[pl.ds(x * self.pitch + here, 1), :]
                    g = []
                    for q in range(4):
                        f_vol = forces[8 * q : 8 * q + 8, self.span(j)]
                        f_dev = forces[32 + 8 * q : 40 + 8 * q, self.span(j)]
                        g.append(vol * f_vol + dev * f_dev)
                    if here >= level:
                        before = None if carried is None else carried[:, self.span(here)]
                        carry_to[:, self.span(here)] = g[2] + side_high
                        emit(x, here, g[0] + side_low, before)
                    side_low, side_high = g[1], g[3]
                z += cols
            carried = carry_to


Refs = collections.namedtuple("Refs", ("tiles", "dev", "keep", "gain", "ahead", "field", "split"))


def gram_tiles(nx, nz, here, w_at, sums):
    for c in range(3):
        for x in range(nx):
            for t in range(nz // 8):
                at = (c * nx + x) * nz + 8 * t
                w = {}
                for n, (i, j) in enumerate(PAIRS):
                    if here(j, x):
                        for level in (i, j):
                            if level not in w:
                                w[level] = w_at(level, x)[at : at + 8, :]
                        term = w[i] * w[j]
                        sums[n] = term if sums[n] is None else sums[n] + term
    return sums


def inner_product_kernel(
    dims,
    load_ref, plastic_ref, modulus_ref, ca_ref, cb_ref, k_ref, scale_ref,
    w0_ref, w1_ref, w2_ref, w3_ref, part_ref, stash_ref,
    tiles_ref, dev_ref, field_ref, split_ref, clow_ref, chigh_ref,
    sum_ref, keep_ref, gain_ref, ahead_ref,
):
    nx, nz, ny, tx, tz, _ = dims
    work = Products(dims, k_ref[...], scale_ref)
    pitch = work.pitch
    refs = Refs(tiles_ref, dev_ref, keep_ref, gain_ref, ahead_ref, field_ref, split_ref)
    w_refs = (w0_ref, w1_ref, w2_ref, w3_ref)
    pick(ca_ref, cb_ref, is_odd("curve"), clow_ref, chigh_ref)
    tiles_ref[...] = jnp.zeros_like(tiles_ref)
    for tile_x in range(tx):
        row = (tile_x + 1) * (tz + 2)
        at = 4 * HALO * nx + tile_x
        tiles_ref[row : row + 1, :] = clow_ref[at : at + 1, :]
        tiles_ref[row + 1 : row + 1 + tz, :] = modulus_ref[tile_x * tz : (tile_x + 1) * tz, :]
        tiles_ref[row + 1 + tz : row + 2 + tz, :] = chigh_ref[at : at + 1, :]
    for own in range(nx):
        x = own + HALO
        inside = 1.0 - plastic_ref[own * nz : (own + 1) * nz, :]
        for t in range(tz):
            row = work.tile_row(x, HALO + t * TILE)
            first = x * pitch + HALO + t * TILE
            part = inside[t * TILE : (t + 1) * TILE, :]
            dev_ref[first : first + TILE, :] = tiles_ref[row : row + 1, :] * part
    for zl in range(HALO):
        at = (3 * HALO + zl) * nx
        for ref, z in ((clow_ref, zl), (chigh_ref, HALO + nz + zl)):
            for tile_x in range(tx):
                row = work.tile_row(HALO + tile_x * TILE, z)
                rows = slice(at + tile_x * TILE, at + (tile_x + 1) * TILE)
                value = tiles_ref[row : row + 1, :] * (1.0 - ref[rows, :])
                dev_ref[pl.ds((HALO + tile_x * TILE) * pitch + z, TILE, stride=pitch), :] = value
    first, last = HALO + 1, HALO + nx - 1
    work.mark_kept(refs, range(first, last + 1))
    for x in range(first, last + 1):
        own = x - HALO
        for z in range(work.size_z):
            if z < HALO:
                rows = clow_ref[pl.ds(z * nx + own, 3, stride=HALO * nx), :]
            elif z >= HALO + nz:
                rows = chigh_ref[pl.ds((z - HALO - nz) * nx + own, 3, stride=HALO * nx), :]
            else:
                rows = load_ref[pl.ds(own * nz + z - HALO, 3, stride=nx * nz), :]
            work.start_node(refs, x, z, rows, w0_ref)
    for level in range(1, ITERS + 1):
        layers = range(HALO + level, HALO + nx - level)
        low_ref, high_ref = stash_ref.at[2 * level - 2], stash_ref.at[2 * level - 1]

        def emit(x, z, total, before, level=level, low_ref=low_ref):
            if before is None:
                low_ref[:, work.span(z)] = total
            else:
                work.update_node(refs, refs, x, z, total + before, w_refs[level])

        work.sweep(
            level, layers[:-1], lambda x: split_ref, lambda x: (tiles_ref, dev_ref), None, emit, sum_ref
        )
        carried = sum_ref if len(layers) > 1 else None
        work.sweep(
            level, layers[-1:], lambda x: split_ref, lambda x: (tiles_ref, dev_ref), carried, emit, high_ref
        )
    sums = gram_tiles(
        nx, nz, lambda j, x: x in inner_rows(nx, j), lambda j, x: w_refs[j], [None] * len(PAIRS)
    )
    for n, value in enumerate(sums):
        part_ref[8 * n : 8 * n + 8, :] = jnp.zeros((8, ny), jnp.float32) if value is None else value


def outer_product_kernel(
    dims,
    modulus_ref, load_ref, sa_ref, sb_ref, k_ref, scale_ref,
    a0_ref, a1_ref, a2_ref, a3_ref, part_ref, stash_ref,
    itiles_ref, idev_ref, ifield_ref, isplit_ref, clow_ref, chigh_ref,
    b0_ref, b1_ref, b2_ref, b3_ref, gram_ref,
    slow_ref, shigh_ref, tiles_ref, dev_ref, keep_ref, gain_ref, ahead_ref, field_ref, split_ref, sum_ref,
):
    nx, nz, ny, tx, tz, _ = dims
    work = Products(dims, k_ref[...], scale_ref)
    pitch, size_x, size_z = work.pitch, work.size_x, work.size_z
    refs = Refs(tiles_ref, dev_ref, keep_ref, gain_ref, ahead_ref, field_ref, split_ref)
    inner = Refs(tiles_ref, idev_ref, keep_ref, gain_ref, ahead_ref, ifield_ref, isplit_ref)
    a_refs = (a0_ref, a1_ref, a2_ref, a3_ref)
    b_refs = (b0_ref, b1_ref, b2_ref, b3_ref)
    pick(sa_ref, sb_ref, is_odd("sub"), slow_ref, shigh_ref)
    own_layers = range(HALO, HALO + nx)
    tiles_ref[...] = itiles_ref[...]
    at = 4 * HALO * size_z
    for side_ref, row in ((slow_ref, 0), (shigh_ref, (tx + 1) * (tz + 2))):
        tiles_ref[row : row + tz + 2, :] = side_ref[at : at + tz + 2, :]
    for x in range(size_x - 1):
        if x in own_layers:
            continue
        side_ref, xl = (slow_ref, x) if x < HALO else (shigh_ref, x - HALO - nx)
        inside = 1.0 - side_ref[(3 * HALO + xl) * size_z : (3 * HALO + xl + 1) * size_z, :]
        bounds = [0, *range(HALO, HALO + nz + 1, TILE), size_z]
        for first, last in zip(bounds, bounds[1:]):
            row = work.tile_row(x, first)
            value = tiles_ref[row : row + 1, :] * inside[first:last, :]
            dev_ref[x * pitch + first : x * pitch + last, :] = value
    started = range(HALO + 1, HALO + nx)
    rest = [x for x in range(size_x) if x not in started]
    work.mark_kept(refs, range(size_x))
    for x in rest:
        for z in range(size_z):
            if x < HALO:
                rows = slow_ref[pl.ds(x * size_z + z, 3, stride=HALO * size_z), :]
            elif x >= HALO + nx:
                rows = shigh_ref[pl.ds((x - HALO - nx) * size_z + z, 3, stride=HALO * size_z), :]
            elif z < HALO:
                rows = clow_ref[pl.ds(z * nx + x - HALO, 3, stride=HALO * nx), :]
            elif z >= HALO + nz:
                rows = chigh_ref[pl.ds((z - HALO - nz) * nx + x - HALO, 3, stride=HALO * nx), :]
            else:
                rows = load_ref[pl.ds((x - HALO) * nz + z - HALO, 3, stride=nx * nz), :]
            work.start_node(refs, x, z, rows, b0_ref)

    held = {x: inner if x in started else refs for x in range(size_x)}

    def update(x, z, total, level):
        work.update_node(refs, held[x], x, z, total, b_refs[level])

    def coefficients_at(x):
        return tiles_ref, (inner if x in own_layers else refs).dev

    for level in range(1, ITERS + 1):
        done = []

        def emit(x, z, total, before, level=level, done=done):
            if before is not None:
                update(x, z, total + before, level)
                done.append(x)

        def split_at(x):
            return held[x].split

        edge = HALO + level
        work.sweep(level, range(level - 1, edge), split_at, coefficients_at, None, emit, sum_ref)
        low_ref, high_ref = stash_ref.at[2 * level - 2], stash_ref.at[2 * level - 1]
        for z in range(level, size_z - level):
            update(edge, z, sum_ref[:, work.span(z)] + low_ref[:, work.span(z)], level)
        done.append(edge)
        upper = range(HALO + nx - level, size_x - level)
        work.sweep(level, upper, split_at, coefficients_at, high_ref, emit, sum_ref)
        for x in set(done):
            held[x] = refs

    sums = [part_ref[8 * n : 8 * n + 8, :] for n in range(len(PAIRS))]
    sums = gram_tiles(
        nx, nz, lambda j, x: x not in inner_rows(nx, j),
        lambda j, x: (a_refs if x in inner_rows(nx, j) else b_refs)[j], sums,
    )
    lane = lax.broadcasted_iota(jnp.int32, (1, ny), 1)
    row = jnp.zeros((1, ny), jnp.float32)
    for n, value in enumerate(sums):
        row = jnp.where(lane == n, jnp.sum(value, axis=(0, 1), keepdims=True), row)
    gram_ref[...] = jnp.broadcast_to(row[None], gram_ref.shape)


def finish_kernel(dims, gram_ref, scale_ref, *refs):
    nx, nz = dims[:2]
    a_refs, b_refs = refs[: ITERS + 1], refs[ITERS + 1 : 2 * ITERS + 2]
    solution_ref, residual_ref, better_ref, poor_ref = refs[2 * ITERS + 2 :]
    total = jnp.sum(gram_ref[...], axis=0)
    lane = lax.broadcasted_iota(jnp.int32, total.shape, 1)
    gram = {}
    for n, (i, j) in enumerate(PAIRS):
        value = jnp.sum(jnp.where(lane == n, total, 0.0), axis=1, keepdims=True)
        gram[i, j] = gram[j, i] = value

    def inner(p, q):
        result = None
        for i, left in enumerate(p):
            for j, right in enumerate(q):
                if left is not None and right is not None:
                    term = left * right * gram[i, j]
                    result = term if result is None else result + term
        return result

    def axpy(p, scale, q):
        out = []
        for left, right in zip(p, q):
            if right is None:
                out.append(left)
            else:
                out.append(scale * right if left is None else left + scale * right)
        return out

    def image_of(p):
        out = []
        for i in range(ITERS + 1):
            here = p[i]
            before = p[i - 1] if i > 0 else None
            if here is None:
                out.append(None if before is None else -before)
            else:
                out.append(here if before is None else here - before)
        return out

    one = jnp.ones((1, 1), jnp.float32)
    solution = [None] * (ITERS + 1)
    residual = [one] + [None] * ITERS
    image = image_of(residual)
    norm_now = inner(residual, residual)
    step = first_step = norm_now / inner(residual, image)
    direction = residual
    carried = image
    for iteration in range(ITERS):
        solution = axpy(solution, step, direction)
        residual = axpy(residual, -step, carried)
        if iteration + 1 < ITERS:
            image = image_of(residual)
            norm_next = inner(residual, residual)
            curvature = inner(residual, image)
            ratio = norm_next / norm_now
            step = norm_next / (curvature - ratio * norm_next / step)
            direction = axpy(residual, ratio, direction)
            carried = axpy(image, ratio, carried)
            norm_now = norm_next
    inverse = scale_ref[0:1, 0:1]
    better_ref[...] = jnp.broadcast_to(first_step * inverse, better_ref.shape)
    solution = [None if c is None else c * inverse for c in solution]
    for x in range(nx):
        for component in range(3):
            rows = slice((component * nx + x) * nz, (component * nx + x + 1) * nz)
            w = [(a_refs if x in inner_rows(nx, j) else b_refs)[j][rows, :] for j in range(ITERS + 1)]
            for out_ref, coefs in ((solution_ref, solution), (residual_ref, residual)):
                value = None
                for c, vector in zip(coefs, w):
                    if c is not None:
                        value = c * vector if value is None else value + c * vector
                out_ref[rows, :] = value
    terms = None
    for i, c in enumerate(residual):
        size = jnp.abs(c) * jnp.sqrt(gram[i, i])
        terms = size if terms is None else terms + size
    well = terms <= MAX_GROWTH * jnp.sqrt(inner(residual, residual))
    poor_ref[0, 0] = jnp.where(jnp.max(jnp.where(well, 0.0, 1.0)) > 0, 1, 0)


def local(load, plastic, tile_material, moduli, k_vol, k_dev):
    nx, nz, ny = plastic.shape
    dims = (nx, nz, ny) + tile_material.shape
    tx, tz = tile_material.shape[:2]
    f32 = jnp.float32
    vmem = pl.BlockSpec(memory_space=pltpu.VMEM)
    smem = pl.BlockSpec(memory_space=pltpu.SMEM)
    shape = jax.ShapeDtypeStruct
    kept = pltpu.VMEM
    grant = pltpu.CompilerParams(vmem_limit_bytes=16 * 2**20)

    def near(*values):
        return [pltpu.with_memory_space_constraint(v, pltpu.VMEM) for v in values]

    def far(*values):
        return [pltpu.with_memory_space_constraint(v, pltpu.HBM) for v in values]

    load = load.reshape(3 * nx * nz, ny)
    plastic = plastic.reshape(nx * nz, ny)
    size_x = nx + 2 * HALO
    size_z = nz + 2 * HALO
    pitch = round_up(size_z, 8)
    curve_rows = round_up(4 * HALO * nx + tx, 8)
    sub_rows = round_up(4 * HALO * size_z + tz + 2, 8)
    count = lax.axis_size("curve") * lax.axis_size("sub")

    curve_a, curve_b, modulus = pl.pallas_call(
        functools.partial(curve_message_kernel, dims),
        out_shape=(kept((curve_rows, ny), f32), kept((curve_rows, ny), f32), kept((round_up(tx * tz, 8), ny), f32)),
        in_specs=[smem, smem, vmem, vmem],
        out_specs=(vmem,) * 3,
        compiler_params=grant,
        name="curve_message",
    )(*far(tile_material, moduli, load, plastic))
    k_both, scale = pl.pallas_call(
        setup_kernel,
        out_shape=(kept((64, 128), jnp.bfloat16), kept((8, 128), f32)),
        in_specs=[smem, vmem, vmem, vmem],
        out_specs=(vmem,) * 2,
        compiler_params=grant,
        name="setup",
    )(*far(moduli), k_vol, k_dev, *near(modulus))
    curve_b = exchange(curve_b, "curve", 1)
    curve_a = exchange(curve_a, "curve", 0)
    sub_a, sub_b = pl.pallas_call(
        functools.partial(sub_message_kernel, dims),
        out_shape=(kept((sub_rows, ny), f32),) * 2,
        in_specs=[vmem] * 6,
        out_specs=(vmem,) * 2,
        scratch_shapes=[pltpu.VMEM((curve_rows, ny), f32)] * 2,
        compiler_params=grant,
        name="sub_message",
    )(*near(load, plastic, modulus, curve_a, curve_b, scale))
    sub_b = exchange(sub_b, "sub", 1)
    sub_a = exchange(sub_a, "sub", 0)
    basis_shape = (kept((3 * nx * nz, ny), f32),) * (ITERS + 1)
    coefficient = (size_x * pitch, ny)
    tile_rows = (round_up((tx + 2) * (tz + 2), 8), ny)
    class_rows = (round_up((2 * tx + 3) * (2 * tz + 3), 8), ny)
    field = (size_x, 8, size_z * ny)
    split = (size_x, 16, size_z * ny)
    stash = (2 * ITERS, 8, size_z * ny)

    def solve(scale):
        *first, part, stashed, tiles, dev, fields, splits, low, high = pl.pallas_call(
            functools.partial(inner_product_kernel, dims),
            out_shape=basis_shape + (
                kept((8 * len(PAIRS), ny), f32), kept(stash, f32),
                kept(tile_rows, f32), kept(coefficient, f32),
                kept(field, f32), kept(split, jnp.bfloat16),
                kept((curve_rows, ny), f32), kept((curve_rows, ny), f32),
            ),
            in_specs=[vmem] * 7,
            out_specs=(vmem,) * (ITERS + 9),
            scratch_shapes=[pltpu.VMEM((8, size_z * ny), f32)] + [pltpu.VMEM(class_rows, f32)] * 3,
            compiler_params=grant,
            name="inner_products",
        )(*near(load, plastic, modulus, curve_a, curve_b, k_both, scale))
        *second, gram = pl.pallas_call(
            functools.partial(outer_product_kernel, dims),
            out_shape=basis_shape + (kept((count, 1, ny), f32),),
            in_specs=[vmem] * (ITERS + 15),
            out_specs=(vmem,) * (ITERS + 2),
            scratch_shapes=[
                pltpu.VMEM((sub_rows, ny), f32), pltpu.VMEM((sub_rows, ny), f32),
                pltpu.VMEM(tile_rows, f32), pltpu.VMEM(coefficient, f32),
                pltpu.VMEM(class_rows, f32), pltpu.VMEM(class_rows, f32), pltpu.VMEM(class_rows, f32),
                pltpu.VMEM(field, f32), pltpu.VMEM(split, jnp.bfloat16),
                pltpu.VMEM((8, size_z * ny), f32),
            ],
            compiler_params=grant,
            name="outer_products",
        )(*near(
            modulus, load, sub_a, sub_b, k_both, scale,
            *first, part, stashed, tiles, dev, fields, splits, low, high,
        ))
        gram = lax.all_to_all(gram, AXES, 0, 0)
        return pl.pallas_call(
            functools.partial(finish_kernel, dims),
            out_shape=(shape((3 * nx * nz, ny), f32),) * 2 + (kept((8, 128), f32), pltpu.SMEM((1, 1), jnp.int32)),
            in_specs=[vmem] * (2 * ITERS + 4),
            out_specs=(vmem, vmem, vmem, smem),
            compiler_params=grant,
            name="finish",
        )(*near(gram, scale, *first, *second))

    *found, better, poor = solve(scale)
    found = lax.cond(poor[0, 0] > 0, lambda: tuple(solve(better)[:2]), lambda: tuple(found))
    return tuple(value.reshape(3, nx, nz, ny) for value in found)


def solution(mesh):
    in_specs = (
        P(None, "sub", "curve", None),
        P("sub", "curve", None),
        P("sub", "curve", None),
        P(),
        P(),
        P(),
    )
    out_specs = (P(None, "sub", "curve", None), P(None, "sub", "curve", None))

    return jax.shard_map(local, mesh=mesh, in_specs=in_specs, out_specs=out_specs, check_vma=False)
```

```python
import collections
import functools

import jax
import jax.numpy as jnp
from jax import lax
from jax.experimental import pallas as pl
from jax.experimental.pallas import tpu as pltpu
from jax.sharding import PartitionSpec as P


TILE = 8
MATERIALS = 4
ITERS = 3
HALO = ITERS

ground_spring = 0.5

AXES = ("curve", "sub")
MAX_GROWTH = 40.0
PAIRS = ((0, 0), (0, 1), (0, 2), (0, 3), (1, 1), (1, 2), (1, 3), (2, 2), (2, 3), (3, 3))


def round_up(value, to):
    return -(-value // to) * to


def exchange(value, axis, first):
    count = lax.axis_size(axis)
    pairs = []
    for i in range(first, count - 1, 2):
        pairs += [(i, i + 1), (i + 1, i)]
    return lax.ppermute(value, axis, pairs)


def is_odd(axis):
    return lax.axis_index(axis) % 2 == 1


def curve_message_kernel(
    dims, tile_ref, moduli_ref, load_ref, plastic_ref, a_ref, b_ref, modulus_ref, load_out_ref, plastic_out_ref
):
    nx, nz, ny, tx, tz, ty = dims
    load_out_ref[...] = load_ref[...]
    plastic_out_ref[...] = plastic_ref[...]
    odd = is_odd("curve")
    lane = lax.broadcasted_iota(jnp.int32, (1, ny), 1) // TILE
    for t in range(tx * tz):
        row = jnp.zeros((1, ny), jnp.float32)
        for y in range(ty):
            material = tile_ref[t // tz, t % tz, y]
            value = jnp.float32(0)
            for m in range(MATERIALS):
                value = jnp.where(material == m + 1, moduli_ref[m], value)
            row = jnp.where(lane == y, value, row)
        modulus_ref[t : t + 1, :] = row
    for out_ref, z_first, tile_z in (
        (a_ref, jnp.where(odd, 0, nz - HALO), jnp.where(odd, 0, tz - 1)),
        (b_ref, jnp.where(odd, nz - HALO, 0), jnp.where(odd, tz - 1, 0)),
    ):
        for f in range(4):
            for zl in range(HALO):
                z = z_first + zl
                at = (f * HALO + zl) * nx
                if f < 3:
                    out_ref[at : at + nx, :] = load_ref[pl.ds(f * nx * nz + z, nx, stride=nz), :]
                else:
                    out_ref[at : at + nx, :] = plastic_ref[pl.ds(z, nx, stride=nz), :]
        for t in range(tx):
            at = 4 * HALO * nx + t
            out_ref[at : at + 1, :] = modulus_ref[pl.ds(t * tz + tile_z, 1), :]


def slots_of(parts):
    return round_up(parts, 2)


def setup_kernel(parts, moduli_ref, kv_ref, kd_ref, _, k_ref, scale_ref):
    r32 = lax.broadcasted_iota(jnp.int32, (32, 24), 0)
    m32 = lax.broadcasted_iota(jnp.int32, (32, 24), 1)
    spread_rows = ((m32 == 6 * (r32 // 8) + r32 % 8) & (r32 % 8 < 6)).astype(jnp.bfloat16)
    shape = (24, k_ref.shape[1])
    width = 32 * slots_of(parts)
    m24 = lax.broadcasted_iota(jnp.int32, shape, 0)
    n24 = lax.broadcasted_iota(jnp.int32, shape, 1)
    slot = n24 % (8 * slots_of(parts)) // 8
    target = (m24 == 6 * (n24 % width // (8 * slots_of(parts))) + n24 % 8) & (n24 % 8 < 6) & (slot < parts)
    dot = functools.partial(jnp.dot, preferred_element_type=jnp.float32)
    for at, ref in ((0, kv_ref), (32, kd_ref)):
        rest = ref[...]
        total = None
        for part in range(parts):
            rounded = rest.astype(jnp.bfloat16)
            rest = rest - rounded.astype(jnp.float32)
            columns = (target & (n24 // width == part)).astype(jnp.bfloat16)
            placed = dot(dot(spread_rows, rounded).astype(jnp.bfloat16), columns)
            total = placed if total is None else total + placed
        k_ref[at : at + 32, :] = total.astype(jnp.bfloat16)

    def size(k):
        top = jnp.max(jnp.abs(k), axis=(0, 1), keepdims=True)
        safe = jnp.where(top > 0, top, 1.0)
        return top * jnp.sqrt(jnp.sum((k / safe) ** 2, axis=(0, 1), keepdims=True) * (1.0 / 24))

    mean_modulus = jnp.float32(0)
    for m in range(MATERIALS):
        mean_modulus = mean_modulus + moduli_ref[m] * (1.0 / MATERIALS)
    theta = ground_spring + 6.6 * mean_modulus * (size(kv_ref[...]) + size(kd_ref[...]))
    scale_ref[...] = jnp.broadcast_to(1.0 / theta, (8, 128))


def pick(ref_a, ref_b, odd, low_ref, high_ref):
    a = ref_a[...]
    b = ref_b[...]
    low_ref[...] = jnp.where(odd, a, b)
    high_ref[...] = jnp.where(odd, b, a)


def sub_message_kernel(dims, load_ref, plastic_ref, modulus_ref, ra_ref, rb_ref, _, a_ref, b_ref, low_ref, high_ref):
    nx, nz, _, tx, tz, _ = dims
    size_z = nz + 2 * HALO
    pick(ra_ref, rb_ref, is_odd("curve"), low_ref, high_ref)
    odd = is_odd("sub")
    for out_ref, x_first, tile_x in (
        (a_ref, jnp.where(odd, 0, nx - HALO), jnp.where(odd, 0, tx - 1)),
        (b_ref, jnp.where(odd, nx - HALO, 0), jnp.where(odd, tx - 1, 0)),
    ):
        for f in range(4):
            for xl in range(HALO):
                at = (f * HALO + xl) * size_z
                x = x_first + xl
                if f < 3:
                    own = load_ref[pl.ds(f * nx * nz + x * nz, nz), :]
                else:
                    own = plastic_ref[pl.ds(x * nz, nz), :]
                side = f * HALO * nx
                out_ref[at : at + HALO, :] = low_ref[pl.ds(side + x, HALO, stride=nx), :]
                out_ref[at + HALO : at + HALO + nz, :] = own
                out_ref[at + HALO + nz : at + size_z, :] = high_ref[pl.ds(side + x, HALO, stride=nx), :]
        at = 4 * HALO * size_z
        out_ref[at : at + 1, :] = low_ref[pl.ds(4 * HALO * nx + tile_x, 1), :]
        out_ref[at + 1 : at + 1 + tz, :] = modulus_ref[pl.ds(tile_x * tz, tz), :]
        out_ref[at + 1 + tz : at + 2 + tz, :] = high_ref[pl.ds(4 * HALO * nx + tile_x, 1), :]


def inner_rows(nx, level):
    return range(1, nx) if level == 0 else range(level + 1, nx - level)


class Products:

    def __init__(self, dims, parts, kmat, scale_ref):
        self.parts = parts
        self.nx, self.nz, self.ny = dims[:3]
        self.size_x = self.nx + 2 * HALO
        self.size_z = self.nz + 2 * HALO
        self.pitch = round_up(self.size_z, 8)
        self.kmat = kmat
        self.component = lax.broadcasted_iota(jnp.int32, (8, self.ny), 0) < 3
        self.inverse = scale_ref[0:1, 0:1]
        self.blank = jnp.zeros((5, self.ny), jnp.float32)

    def span(self, z):
        return slice(z * self.ny, (z + 1) * self.ny)

    def tile(self, index):
        return (index // TILE + 1)

    def tile_row(self, x, z):
        return self.tile(x - HALO) * (self.nz // TILE + 2) + self.tile(z - HALO)

    def node_class(self, index):
        return self.tile(index - HALO - 1), self.tile(index - HALO)

    def mark_kept(self, refs, layers):
        self.rows = {}
        rows = refs.tiles.shape[0]
        lane = lax.broadcasted_iota(jnp.int32, (1, self.ny), 1)
        own, ahead = [], []
        for at in range(0, rows, 8):
            e = refs.tiles[at : at + 8, :]
            own.append(jnp.maximum(e, pltpu.roll(e, 1, 1)))
            ahead.append(jnp.maximum(e, pltpu.roll(e, self.ny - 1, 1)))
        own = jnp.concatenate(own, axis=0)
        ahead = jnp.concatenate(ahead, axis=0)
        per_x = self.nz // TILE + 2
        x_index = lax.axis_index("sub") * self.nx - HALO
        x_count = lax.axis_size("sub") * self.nx
        z_index = lax.axis_index("curve") * self.nz - HALO
        z_count = lax.axis_size("curve") * self.nz
        for x in layers:
            for z in range(self.size_z):
                key = self.node_class(x), self.node_class(z)
                if key in self.rows:
                    continue
                n = self.rows[key] = len(self.rows)
                free = (x_index + x > 0) & (x_index + x < x_count) & (z_index + z > 0) & (z_index + z < z_count)
                free = jnp.where(free, 1.0, 0.0)
                around = sorted({tx * per_x + tz for tx in key[0] for tz in key[1]})
                kept = []
                for e, inside in ((own, lane > 0), (ahead, lane < self.ny - 1)):
                    top = functools.reduce(jnp.maximum, [e[r : r + 1, :] for r in around])
                    kept.append(jnp.where(inside & (top > 0), free, 0.0))
                refs.keep[n : n + 1, :] = kept[0]
                refs.gain[n : n + 1, :] = kept[0] * self.inverse
                refs.ahead[n : n + 1, :] = kept[1] * self.inverse

    def kept_row(self, ref, x, z):
        n = self.rows[self.node_class(x), self.node_class(z)]
        return ref[n : n + 1, :]

    def store_node(self, refs, x, z, both, w_ref):
        span = self.span(z)
        refs.field[x, :, span] = both
        pieces, rest = [], both
        for _ in range(self.parts - 1):
            pieces.append(rest.astype(jnp.bfloat16).astype(jnp.float32))
            rest = rest - pieces[-1]
        pieces.append(rest)
        pieces += [jnp.zeros_like(both)] * (slots_of(self.parts) - self.parts)
        refs.split[x, :, span] = jnp.concatenate(pieces, axis=0).astype(jnp.bfloat16)
        own_x, own_z = x - HALO, z - HALO
        if 0 <= own_x < self.nx and 0 <= own_z < self.nz:
            w_ref[pl.ds(own_x * self.nz + own_z, 3, stride=self.nx * self.nz), :] = both[0:3, :]

    def start_node(self, refs, x, z, rows, w_ref):
        value = jnp.concatenate([rows, self.blank], axis=0) * self.kept_row(refs.keep, x, z)
        ahead = pltpu.roll(pltpu.roll(value, self.ny - 1, 1), 3, 0)
        self.store_node(refs, x, z, value + ahead, w_ref)

    def update_node(self, refs, held, x, z, total, w_ref):
        below = pltpu.roll(pltpu.roll(total, 1, 1), 5, 0)
        above = pltpu.roll(pltpu.roll(total, self.ny - 1, 1), 3, 0)
        total = total + jnp.where(self.component, below, above)
        old = held.field[x, :, self.span(z)]
        gain = jnp.where(self.component, self.kept_row(refs.gain, x, z), self.kept_row(refs.ahead, x, z))
        self.store_node(refs, x, z, old - gain * (total + ground_spring * old), w_ref)

    def sweep(self, level, layers, split_at, coefficients_at, carried, emit, carry_to):
        for x in layers:
            tiles_ref, dev_ref = coefficients_at(x)
            z, end = level - 1, self.size_z - level
            side_low = side_high = None
            while z < end:
                cols = min(2, end - z)
                lanes = cols * self.ny
                corners = []
                for a in (0, 1):
                    source = split_at(x + a)
                    for c in (0, 1):
                        corners.append(source[x + a, :, (z + c) * self.ny : (z + c) * self.ny + lanes])
                rhs = jnp.concatenate(corners * self.parts, axis=0)
                forces = jnp.dot(self.kmat, rhs, preferred_element_type=jnp.float32)
                for j in range(cols):
                    here = z + j
                    row = self.tile_row(x, here)
                    vol = tiles_ref[row : row + 1, :]
                    dev = dev_ref[pl.ds(x * self.pitch + here, 1), :]
                    g = []
                    for q in range(4):
                        f_vol = forces[8 * q : 8 * q + 8, self.span(j)]
                        f_dev = forces[32 + 8 * q : 40 + 8 * q, self.span(j)]
                        g.append(vol * f_vol + dev * f_dev)
                    if here >= level:
                        before = None if carried is None else carried[:, self.span(here)]
                        carry_to[:, self.span(here)] = g[2] + side_high
                        emit(x, here, g[0] + side_low, before)
                    side_low, side_high = g[1], g[3]
                z += cols
            carried = carry_to


Refs = collections.namedtuple("Refs", ("tiles", "dev", "keep", "gain", "ahead", "field", "split"))


def gram_tiles(nx, nz, here, w_at, sums):
    for c in range(3):
        for x in range(nx):
            for t in range(nz // 8):
                at = (c * nx + x) * nz + 8 * t
                w = {}
                for n, (i, j) in enumerate(PAIRS):
                    if here(j, x):
                        for level in (i, j):
                            if level not in w:
                                w[level] = w_at(level, x)[at : at + 8, :]
                        term = w[i] * w[j]
                        sums[n] = term if sums[n] is None else sums[n] + term
    return sums


def inner_product_kernel(
    dims, parts,
    load_ref, plastic_ref, modulus_ref, ca_ref, cb_ref, k_ref, scale_ref,
    w0_ref, w1_ref, w2_ref, w3_ref, part_ref, stash_ref,
    tiles_ref, dev_ref, field_ref, split_ref, clow_ref, chigh_ref,
    sum_ref, keep_ref, gain_ref, ahead_ref,
):
    nx, nz, ny, tx, tz, _ = dims
    work = Products(dims, parts, k_ref[...], scale_ref)
    pitch = work.pitch
    refs = Refs(tiles_ref, dev_ref, keep_ref, gain_ref, ahead_ref, field_ref, split_ref)
    w_refs = (w0_ref, w1_ref, w2_ref, w3_ref)
    pick(ca_ref, cb_ref, is_odd("curve"), clow_ref, chigh_ref)
    tiles_ref[...] = jnp.zeros_like(tiles_ref)
    for tile_x in range(tx):
        row = (tile_x + 1) * (tz + 2)
        at = 4 * HALO * nx + tile_x
        tiles_ref[row : row + 1, :] = clow_ref[at : at + 1, :]
        tiles_ref[row + 1 : row + 1 + tz, :] = modulus_ref[tile_x * tz : (tile_x + 1) * tz, :]
        tiles_ref[row + 1 + tz : row + 2 + tz, :] = chigh_ref[at : at + 1, :]
    for own in range(nx):
        x = own + HALO
        inside = 1.0 - plastic_ref[own * nz : (own + 1) * nz, :]
        for t in range(tz):
            row = work.tile_row(x, HALO + t * TILE)
            first = x * pitch + HALO + t * TILE
            part = inside[t * TILE : (t + 1) * TILE, :]
            dev_ref[first : first + TILE, :] = tiles_ref[row : row + 1, :] * part
    for zl in range(HALO):
        at = (3 * HALO + zl) * nx
        for ref, z in ((clow_ref, zl), (chigh_ref, HALO + nz + zl)):
            for tile_x in range(tx):
                row = work.tile_row(HALO + tile_x * TILE, z)
                rows = slice(at + tile_x * TILE, at + (tile_x + 1) * TILE)
                value = tiles_ref[row : row + 1, :] * (1.0 - ref[rows, :])
                dev_ref[pl.ds((HALO + tile_x * TILE) * pitch + z, TILE, stride=pitch), :] = value
    first, last = HALO + 1, HALO + nx - 1
    work.mark_kept(refs, range(first, last + 1))
    for x in range(first, last + 1):
        own = x - HALO
        for z in range(work.size_z):
            if z < HALO:
                rows = clow_ref[pl.ds(z * nx + own, 3, stride=HALO * nx), :]
            elif z >= HALO + nz:
                rows = chigh_ref[pl.ds((z - HALO - nz) * nx + own, 3, stride=HALO * nx), :]
            else:
                rows = load_ref[pl.ds(own * nz + z - HALO, 3, stride=nx * nz), :]
            work.start_node(refs, x, z, rows, w0_ref)
    for level in range(1, ITERS + 1):
        layers = range(HALO + level, HALO + nx - level)
        low_ref, high_ref = stash_ref.at[2 * level - 2], stash_ref.at[2 * level - 1]

        def emit(x, z, total, before, level=level, low_ref=low_ref):
            if before is None:
                low_ref[:, work.span(z)] = total
            else:
                work.update_node(refs, refs, x, z, total + before, w_refs[level])

        work.sweep(
            level, layers[:-1], lambda x: split_ref, lambda x: (tiles_ref, dev_ref), None, emit, sum_ref
        )
        carried = sum_ref if len(layers) > 1 else None
        work.sweep(
            level, layers[-1:], lambda x: split_ref, lambda x: (tiles_ref, dev_ref), carried, emit, high_ref
        )
    sums = gram_tiles(
        nx, nz, lambda j, x: x in inner_rows(nx, j), lambda j, x: w_refs[j], [None] * len(PAIRS)
    )
    for n, value in enumerate(sums):
        part_ref[8 * n : 8 * n + 8, :] = jnp.zeros((8, ny), jnp.float32) if value is None else value


def outer_product_kernel(
    dims, parts,
    modulus_ref, load_ref, sa_ref, sb_ref, k_ref, scale_ref,
    a0_ref, a1_ref, a2_ref, a3_ref, part_ref, stash_ref,
    itiles_ref, idev_ref, ifield_ref, isplit_ref, clow_ref, chigh_ref,
    b0_ref, b1_ref, b2_ref, b3_ref, gram_ref,
    slow_ref, shigh_ref, tiles_ref, dev_ref, keep_ref, gain_ref, ahead_ref, field_ref, split_ref, sum_ref,
):
    nx, nz, ny, tx, tz, _ = dims
    work = Products(dims, parts, k_ref[...], scale_ref)
    pitch, size_x, size_z = work.pitch, work.size_x, work.size_z
    refs = Refs(tiles_ref, dev_ref, keep_ref, gain_ref, ahead_ref, field_ref, split_ref)
    inner = Refs(tiles_ref, idev_ref, keep_ref, gain_ref, ahead_ref, ifield_ref, isplit_ref)
    a_refs = (a0_ref, a1_ref, a2_ref, a3_ref)
    b_refs = (b0_ref, b1_ref, b2_ref, b3_ref)
    pick(sa_ref, sb_ref, is_odd("sub"), slow_ref, shigh_ref)
    own_layers = range(HALO, HALO + nx)
    tiles_ref[...] = itiles_ref[...]
    at = 4 * HALO * size_z
    for side_ref, row in ((slow_ref, 0), (shigh_ref, (tx + 1) * (tz + 2))):
        tiles_ref[row : row + tz + 2, :] = side_ref[at : at + tz + 2, :]
    for x in range(size_x - 1):
        if x in own_layers:
            continue
        side_ref, xl = (slow_ref, x) if x < HALO else (shigh_ref, x - HALO - nx)
        inside = 1.0 - side_ref[(3 * HALO + xl) * size_z : (3 * HALO + xl + 1) * size_z, :]
        bounds = [0, *range(HALO, HALO + nz + 1, TILE), size_z]
        for first, last in zip(bounds, bounds[1:]):
            row = work.tile_row(x, first)
            value = tiles_ref[row : row + 1, :] * inside[first:last, :]
            dev_ref[x * pitch + first : x * pitch + last, :] = value
    started = range(HALO + 1, HALO + nx)
    rest = [x for x in range(size_x) if x not in started]
    work.mark_kept(refs, range(size_x))
    for x in rest:
        for z in range(size_z):
            if x < HALO:
                rows = slow_ref[pl.ds(x * size_z + z, 3, stride=HALO * size_z), :]
            elif x >= HALO + nx:
                rows = shigh_ref[pl.ds((x - HALO - nx) * size_z + z, 3, stride=HALO * size_z), :]
            elif z < HALO:
                rows = clow_ref[pl.ds(z * nx + x - HALO, 3, stride=HALO * nx), :]
            elif z >= HALO + nz:
                rows = chigh_ref[pl.ds((z - HALO - nz) * nx + x - HALO, 3, stride=HALO * nx), :]
            else:
                rows = load_ref[pl.ds((x - HALO) * nz + z - HALO, 3, stride=nx * nz), :]
            work.start_node(refs, x, z, rows, b0_ref)

    held = {x: inner if x in started else refs for x in range(size_x)}

    def update(x, z, total, level):
        work.update_node(refs, held[x], x, z, total, b_refs[level])

    def coefficients_at(x):
        return tiles_ref, (inner if x in own_layers else refs).dev

    for level in range(1, ITERS + 1):
        done = []

        def emit(x, z, total, before, level=level, done=done):
            if before is not None:
                update(x, z, total + before, level)
                done.append(x)

        def split_at(x):
            return held[x].split

        edge = HALO + level
        work.sweep(level, range(level - 1, edge), split_at, coefficients_at, None, emit, sum_ref)
        low_ref, high_ref = stash_ref.at[2 * level - 2], stash_ref.at[2 * level - 1]
        for z in range(level, size_z - level):
            update(edge, z, sum_ref[:, work.span(z)] + low_ref[:, work.span(z)], level)
        done.append(edge)
        upper = range(HALO + nx - level, size_x - level)
        work.sweep(level, upper, split_at, coefficients_at, high_ref, emit, sum_ref)
        for x in set(done):
            held[x] = refs

    sums = [part_ref[8 * n : 8 * n + 8, :] for n in range(len(PAIRS))]
    sums = gram_tiles(
        nx, nz, lambda j, x: x not in inner_rows(nx, j),
        lambda j, x: (a_refs if x in inner_rows(nx, j) else b_refs)[j], sums,
    )
    rows = [jnp.sum(value, axis=0, keepdims=True) for value in sums]
    rows.append(jnp.zeros((round_up(len(PAIRS), 8) - len(PAIRS), ny), jnp.float32))
    total = jnp.sum(jnp.concatenate(rows, axis=0), axis=1, keepdims=True)
    shape = (total.shape[0], ny)
    chosen = lax.broadcasted_iota(jnp.int32, shape, 0) == lax.broadcasted_iota(jnp.int32, shape, 1)
    row = jnp.sum(jnp.where(chosen, total, 0.0), axis=0, keepdims=True)
    gram_ref[...] = jnp.broadcast_to(row[None], gram_ref.shape)


def finish_kernel(dims, gram_ref, scale_ref, *refs):
    nx, nz = dims[:2]
    a_refs, b_refs = refs[: ITERS + 1], refs[ITERS + 1 : 2 * ITERS + 2]
    solution_ref, residual_ref, better_ref, poor_ref = refs[2 * ITERS + 2 :]
    total = jnp.sum(gram_ref[...], axis=0)
    lane = lax.broadcasted_iota(jnp.int32, total.shape, 1)
    gram = {}
    for n, (i, j) in enumerate(PAIRS):
        value = jnp.sum(jnp.where(lane == n, total, 0.0), axis=1, keepdims=True)
        gram[i, j] = gram[j, i] = value

    def inner(p, q):
        result = None
        for i, left in enumerate(p):
            for j, right in enumerate(q):
                if left is not None and right is not None:
                    term = left * right * gram[i, j]
                    result = term if result is None else result + term
        return result

    def axpy(p, scale, q):
        out = []
        for left, right in zip(p, q):
            if right is None:
                out.append(left)
            else:
                out.append(scale * right if left is None else left + scale * right)
        return out

    def image_of(p):
        out = []
        for i in range(ITERS + 1):
            here = p[i]
            before = p[i - 1] if i > 0 else None
            if here is None:
                out.append(None if before is None else -before)
            else:
                out.append(here if before is None else here - before)
        return out

    one = jnp.ones((1, 1), jnp.float32)
    solution = [None] * (ITERS + 1)
    residual = [one] + [None] * ITERS
    image = image_of(residual)
    norm_now = inner(residual, residual)
    step = first_step = norm_now / inner(residual, image)
    direction = residual
    carried = image
    for iteration in range(ITERS):
        solution = axpy(solution, step, direction)
        residual = axpy(residual, -step, carried)
        if iteration + 1 < ITERS:
            image = image_of(residual)
            norm_next = inner(residual, residual)
            curvature = inner(residual, image)
            ratio = norm_next / norm_now
            step = norm_next / (curvature - ratio * norm_next / step)
            direction = axpy(residual, ratio, direction)
            carried = axpy(image, ratio, carried)
            norm_now = norm_next
    inverse = scale_ref[0:1, 0:1]
    better_ref[...] = jnp.broadcast_to(first_step * inverse, better_ref.shape)
    solution = [None if c is None else c * inverse for c in solution]
    for x in range(nx):
        for component in range(3):
            rows = slice((component * nx + x) * nz, (component * nx + x + 1) * nz)
            w = [(a_refs if x in inner_rows(nx, j) else b_refs)[j][rows, :] for j in range(ITERS + 1)]
            for out_ref, coefs in ((solution_ref, solution), (residual_ref, residual)):
                value = None
                for c, vector in zip(coefs, w):
                    if c is not None:
                        value = c * vector if value is None else value + c * vector
                out_ref[rows, :] = value
    terms = None
    for i, c in enumerate(residual):
        size = jnp.abs(c) * jnp.sqrt(gram[i, i])
        terms = size if terms is None else terms + size
    well = terms <= MAX_GROWTH * jnp.sqrt(inner(residual, residual))
    poor_ref[0, 0] = jnp.where(jnp.max(jnp.where(well, 0.0, 1.0)) > 0, 1, 0)


def local(load, plastic, tile_material, moduli, k_vol, k_dev):
    nx, nz, ny = plastic.shape
    dims = (nx, nz, ny) + tile_material.shape
    tx, tz = tile_material.shape[:2]
    f32 = jnp.float32
    vmem = pl.BlockSpec(memory_space=pltpu.VMEM)
    smem = pl.BlockSpec(memory_space=pltpu.SMEM)
    shape = jax.ShapeDtypeStruct
    kept = pltpu.VMEM
    grant = pltpu.CompilerParams(vmem_limit_bytes=16 * 2**20)

    def near(*values):
        return [pltpu.with_memory_space_constraint(v, pltpu.VMEM) for v in values]

    def far(*values):
        return [pltpu.with_memory_space_constraint(v, pltpu.HBM) for v in values]

    load = load.reshape(3 * nx * nz, ny)
    plastic = plastic.reshape(nx * nz, ny)
    size_x = nx + 2 * HALO
    size_z = nz + 2 * HALO
    pitch = round_up(size_z, 8)
    curve_rows = round_up(4 * HALO * nx + tx, 8)
    sub_rows = round_up(4 * HALO * size_z + tz + 2, 8)
    count = lax.axis_size("curve") * lax.axis_size("sub")

    curve_a, curve_b, modulus, load, plastic = pl.pallas_call(
        functools.partial(curve_message_kernel, dims),
        out_shape=(
            kept((curve_rows, ny), f32), kept((curve_rows, ny), f32), kept((round_up(tx * tz, 8), ny), f32),
            kept(load.shape, f32), kept(plastic.shape, f32),
        ),
        in_specs=[smem, smem, vmem, vmem],
        out_specs=(vmem,) * 5,
        compiler_params=grant,
        name="curve_message",
    )(*far(tile_material, moduli, load, plastic))

    def setup(parts):
        return pl.pallas_call(
            functools.partial(setup_kernel, parts),
            out_shape=(kept((64, 32 * slots_of(parts) * parts), jnp.bfloat16), kept((8, 128), f32)),
            in_specs=[smem, vmem, vmem, vmem],
            out_specs=(vmem,) * 2,
            compiler_params=grant,
            name="setup",
        )(*far(moduli, k_vol, k_dev), *near(modulus))

    matrix, scale = setup(2)
    curve_b = exchange(curve_b, "curve", 1)
    curve_a = exchange(curve_a, "curve", 0)
    sub_a, sub_b = pl.pallas_call(
        functools.partial(sub_message_kernel, dims),
        out_shape=(kept((sub_rows, ny), f32),) * 2,
        in_specs=[vmem] * 6,
        out_specs=(vmem,) * 2,
        scratch_shapes=[pltpu.VMEM((curve_rows, ny), f32)] * 2,
        compiler_params=grant,
        name="sub_message",
    )(*near(load, plastic, modulus, curve_a, curve_b, scale))
    sub_b = exchange(sub_b, "sub", 1)
    sub_a = exchange(sub_a, "sub", 0)
    basis_shape = (kept((3 * nx * nz, ny), f32),) * (ITERS + 1)
    coefficient = (size_x * pitch, ny)
    tile_rows = (round_up((tx + 2) * (tz + 2), 8), ny)
    class_rows = (round_up((2 * tx + 3) * (2 * tz + 3), 8), ny)
    field = (size_x, 8, size_z * ny)
    stash = (2 * ITERS, 8, size_z * ny)

    def solve(parts, k_both, scale):
        split = (size_x, 8 * slots_of(parts), size_z * ny)
        *first, part, stashed, tiles, dev, fields, splits, low, high = pl.pallas_call(
            functools.partial(inner_product_kernel, dims, parts),
            out_shape=basis_shape + (
                kept((8 * len(PAIRS), ny), f32), kept(stash, f32),
                kept(tile_rows, f32), kept(coefficient, f32),
                kept(field, f32), kept(split, jnp.bfloat16),
                kept((curve_rows, ny), f32), kept((curve_rows, ny), f32),
            ),
            in_specs=[vmem] * 7,
            out_specs=(vmem,) * (ITERS + 9),
            scratch_shapes=[pltpu.VMEM((8, size_z * ny), f32)] + [pltpu.VMEM(class_rows, f32)] * 3,
            compiler_params=grant,
            name="inner_products",
        )(*near(load, plastic, modulus, curve_a, curve_b, k_both, scale))
        *second, gram = pl.pallas_call(
            functools.partial(outer_product_kernel, dims, parts),
            out_shape=basis_shape + (kept((count, 1, ny), f32),),
            in_specs=[vmem] * (ITERS + 15),
            out_specs=(vmem,) * (ITERS + 2),
            scratch_shapes=[
                pltpu.VMEM((sub_rows, ny), f32), pltpu.VMEM((sub_rows, ny), f32),
                pltpu.VMEM(tile_rows, f32), pltpu.VMEM(coefficient, f32),
                pltpu.VMEM(class_rows, f32), pltpu.VMEM(class_rows, f32), pltpu.VMEM(class_rows, f32),
                pltpu.VMEM(field, f32), pltpu.VMEM(split, jnp.bfloat16),
                pltpu.VMEM((8, size_z * ny), f32),
            ],
            compiler_params=pltpu.CompilerParams(vmem_limit_bytes=16 * 2**20),
            name="outer_products",
        )(*near(
            modulus, load, sub_a, sub_b, k_both, scale,
            *first, part, stashed, tiles, dev, fields, splits, low, high,
        ))
        gram = lax.all_to_all(gram, AXES, 0, 0)
        return pl.pallas_call(
            functools.partial(finish_kernel, dims),
            out_shape=(shape((3 * nx * nz, ny), f32),) * 2 + (kept((8, 128), f32), pltpu.SMEM((1, 1), jnp.int32)),
            in_specs=[vmem] * (2 * ITERS + 4),
            out_specs=(vmem, vmem, vmem, smem),
            compiler_params=grant,
            name="finish",
        )(*near(gram, scale, *first, *second))

    *found, better, poor = solve(2, matrix, scale)
    found = lax.cond(
        poor[0, 0] > 0, lambda: tuple(solve(3, setup(3)[0], better)[:2]), lambda: tuple(found)
    )
    return tuple(value.reshape(3, nx, nz, ny) for value in found)


def solution(mesh):
    in_specs = (
        P(None, "sub", "curve", None),
        P("sub", "curve", None),
        P("sub", "curve", None),
        P(),
        P(),
        P(),
    )
    out_specs = (P(None, "sub", "curve", None), P(None, "sub", "curve", None))

    return jax.shard_map(local, mesh=mesh, in_specs=in_specs, out_specs=out_specs, check_vma=False)
```
